256 devices in a mesh: acq: 16 (over y, x_lo, core), strip: 16 (over x_hi, z).
Axes of the slice: x: 4 (x_hi: 2, x_lo: 2; x = x_hi * 2 + x_lo), y: 4, z: 8, core: 2. Of those that a mesh axis runs over, the one named last changes fastest.
Arguments:
- raw_echoes: float32 [16, 2, 1024, 2048], P('acq', None, 'strip'), may hold values from -6 to 6
- range_filter: float32 [2, 2048], replicated, may hold values from -5 to 5
- azimuth_filter: float32 [2, 1024, 2048], P(None, None, 'strip'), may hold values from -5 to 5
- pair_mask: int32 [16, 2], P('acq'), may hold values 0 or 1
- inversion: float32 [16, 16, 2], P(None, 'acq'), may hold values from -1.5 to 1.5
Outputs:
- epoch_gradients: float32 [16, 2, 512, 256], P('acq', None, 'strip')
The draws below stay inside these ranges and needn't reach their ends.
Inputs may be any that keep to these rules, and one draw needn't show every extreme that they name: `pair_mask`: 1 where the pair is in the network, 0 where it is not.
All inputs are finite; a program needn't handle non-finite values. No bound on the sum of `pair_mask` on one device may be relied on, other than what follows from the above.
Results may differ from the reference program's by a relative error of at most 0.00014.
Values sent between devices are 32-bit elements; how exact they have to be, the bound alone decides.
A program may use at most 64 MiB of HBM per device.

```python
import jax
import jax.numpy as jnp
from jax import lax

NA = 1024
NR = 2048
LOOK = 4
EPOCHS = 16


def set_ends(drawn, rng, smallest, high):
    extent = drawn.shape
    index_at = [jax.random.randint(jax.random.fold_in(rng, axis), (), 0, extent[axis]) for axis in range(len(extent))]
    drawn = drawn.at[tuple(index_at)].set(smallest)
    longest = extent.index(max(extent))
    index_at[longest] = (index_at[longest] + 1) % extent[longest]
    return drawn.at[tuple(index_at)].set(high)


def strengthened(drawn, rng, source, target, shards_of, factor):
    def block_of(axis_at):
        return (jnp.arange(drawn.shape[axis_at]) // (drawn.shape[axis_at] // shards_of)).reshape((-1,) + (1,) * (drawn.ndim - 1 - axis_at))

    first = jax.random.permutation(rng, shards_of)[block_of(target)]
    second = (block_of(target) + shards_of // 2) % shards_of
    return jnp.where((block_of(source) == first) | (block_of(source) == second), factor * drawn, drawn)


def levels(own_key, shape, shards, low, high):
    level = 1.0
    for axis_at, blocks in shards:
        draws = jax.random.uniform(jax.random.fold_in(jax.random.fold_in(own_key, 6), axis_at), (blocks,), jnp.float32, low / len(shards), high / len(shards))
        level = level * jnp.repeat(jnp.exp(draws), shape[axis_at] // blocks).reshape((-1,) + (1,) * (len(shape) - 1 - axis_at))
    return level


def gaussian(rng, extent, spread, bound, shards=(), kind=jnp.bfloat16):
    drawn = spread * jax.random.normal(rng, extent, jnp.float32)
    if shards:
        drawn = drawn * levels(rng, extent, shards, -0.22, 0.18)
    return jnp.clip(drawn, -bound, bound).astype(kind)


def noise_with(rng, shape, width, bound, shards, heavy, held_as=jnp.bfloat16):
    drawn = width * jax.random.normal(rng, shape, jnp.float32)
    if shards:
        drawn = drawn * levels(rng, shape, shards, -0.22, 0.18)
    return jnp.clip(strengthened(drawn, jax.random.fold_in(rng, 3), *heavy), -bound, bound).astype(held_as)


def setup_inputs(seed: int = 0) -> dict:
    keys = jax.random.split(jax.random.key(seed), 6)
    return {
        "raw_echoes": gaussian(keys[0], (EPOCHS, 2, NA, NR), 1.0, 6.0, ((0, 16), (2, 16)), jnp.float32),
        "range_filter": gaussian(keys[1], (2, NR), 0.7071, 5.0, (), jnp.float32),
        "azimuth_filter": gaussian(keys[2], (2, NA, NR), 0.7071, 5.0, ((2, 16),), jnp.float32),
        "pair_mask": set_ends((jax.random.randint(keys[3], (EPOCHS, 2), 0, 4) < 3).astype(jnp.int32), jax.random.fold_in(keys[3], 1), 0, 1),
        "inversion": noise_with(keys[4], (EPOCHS, EPOCHS, 2), (2 * EPOCHS) ** -0.5, 1.5, ((1, 16),), (1, 0, 16, 2.0), jnp.float32),
    }


def multilook(field):
    rows, cols = field.shape
    summed = field.reshape(rows // LOOK, LOOK, cols // LOOK, LOOK).sum(axis=(1, 3)) / LOOK
    return summed.T


def reference(raw_echoes, range_filter, azimuth_filter, pair_mask, inversion):
    range_spec = lax.complex(range_filter[0], range_filter[1])
    azimuth_spec = lax.complex(azimuth_filter[0], azimuth_filter[1])

    def focus(single):
        echo = lax.complex(single[0], single[1])
        compressed = jnp.fft.ifft(jnp.fft.fft(echo, axis=1) * range_spec[None, :], axis=1)
        return jnp.fft.ifft(jnp.fft.fft(compressed, axis=0) * azimuth_spec, axis=0)

    scenes = lax.map(focus, raw_echoes)

    def pair_slopes(later_index):
        later = scenes[later_index]
        slopes = []
        for lag in (1, 2):
            earlier = scenes[jnp.maximum(later_index - lag, 0)]
            product = earlier * jnp.conj(later)
            looked = lax.complex(multilook(jnp.real(product)), multilook(jnp.imag(product)))
            along_azimuth = jnp.imag(looked[:, 1:] * jnp.conj(looked[:, :-1]))
            along_azimuth = jnp.pad(along_azimuth, ((0, 0), (0, 1)))
            along_range = jnp.imag(looked[1:, :] * jnp.conj(looked[:-1, :]))
            along_range = jnp.pad(along_range, ((0, 1), (0, 0)))
            slopes.append(jnp.stack([along_azimuth, along_range]))
        return jnp.stack(slopes)

    epochs = raw_echoes.shape[0]
    slope = lax.map(pair_slopes, jnp.arange(epochs, dtype=jnp.int32))
    lags = jnp.array([1, 2], dtype=jnp.int32)
    usable = pair_mask.astype(jnp.float32) * (jnp.arange(epochs, dtype=jnp.int32)[:, None] >= lags[None, :]).astype(jnp.float32)
    weights = inversion.astype(jnp.float32) * usable[None, :, :]
    return jnp.einsum('ejl,jldra->edra', weights, slope.astype(jnp.float32), precision=lax.Precision.HIGHEST)
```

```python
import functools
import math

import jax
import jax.numpy as jnp
import numpy as np
from jax import lax
from jax.experimental import pallas as pl
from jax.experimental.pallas import tpu as pltpu
from jax.sharding import PartitionSpec as P

MESH = pl.DeviceIdType.MESH
EXACT = lax.Precision.HIGHEST
F32 = jnp.float32
LANES = 128
DEV = 16
Q = 64
CHUNKS = 4
WIDE = 32
PAIRS = [(1, j) for j in range(1, DEV)] + [(2, j) for j in range(2, DEV)]
ROWS = 8 * len(PAIRS)


def block_table(size, sign, scale=1.0):
    index = np.arange(size)
    angle = sign * 2.0 * math.pi / size * (index[:, None] * index[None, :] % size)
    cosine, sine = np.cos(angle) * scale, np.sin(angle) * scale
    return np.block([[cosine, sine], [-sine, cosine]])


def turn_table(count, width, size, sign):
    angle = sign * 2.0 * math.pi / size * (np.arange(count)[:, None] * np.arange(width)[None, :] % size)
    return np.cos(angle), np.sin(angle)


def sample_order():
    order = np.zeros(LANES, dtype=np.int64)
    for h in range(CHUNKS):
        for m in range(4):
            for k in range(8):
                order[WIDE * h + 8 * m + k] = WIDE * h + 4 * k + m
    return order


def tables():
    order = sample_order()
    w1 = block_table(128, -1.0)
    w2 = block_table(128, 1.0, 1.0 / 2048)
    w2 = w2[:, np.concatenate([order, 128 + order])]
    c1, s1 = turn_table(16, 128, 2048, -1.0)
    c2, s2 = turn_table(16, 128, 2048, 1.0)
    turn_range = np.concatenate([c1, s1, c2[:, order], s2[:, order]])
    w3 = block_table(64, -1.0)
    w4 = block_table(64, 1.0, 1.0 / 1024)
    c3, s3 = turn_table(16, 64, 1024, -1.0)
    c4, s4 = turn_table(16, 64, 1024, 1.0)
    turn_pulse = np.concatenate(
        [np.hstack([c3, c3]), np.hstack([-s3, s3]), np.hstack([c4, c4]), np.hstack([-s4, s4])]
    )
    pool = np.zeros((CHUNKS, 256, LANES))
    for h in range(CHUNKS):
        for q in range(Q):
            real, imag = 16 * h + q // 4, 64 + 16 * h + q // 4
            pool[h, q, real] = 0.25
            pool[h, 64 + q, real] = 0.25
            pool[h, 128 + q, imag] = -0.25
            pool[h, 192 + q, imag] = 0.25
    place = np.zeros((8, 32, 256))
    for m in range(8):
        for c in range(2):
            for k in range(16):
                place[m, 16 * c + k, 128 * c + 8 * k + m] = 1.0
    pick = np.zeros((LANES, LANES))
    pick[np.arange(LANES), order] = 1.0
    def split(w):
        high = np.asarray(w, np.float32).astype(jnp.bfloat16)
        return high, (w - high.astype(np.float64)).astype(np.float32).astype(jnp.bfloat16)

    def stacked(w):
        high, low = split(w)
        return np.concatenate([high, high, low])

    def squared(w):
        both = np.concatenate(split(w), axis=1)
        return np.concatenate([both, both])

    pool = np.concatenate([pool, pool], axis=1).reshape(-1, LANES).astype(jnp.bfloat16)
    single = [np.asarray(t, np.float32) for t in (turn_range, turn_pulse, place.reshape(-1, 256), pick, np.eye(LANES))]
    turn_range, turn_pulse, place, pick, eye = single
    return [stacked(w1), stacked(w2), turn_range, squared(w3), squared(w4), turn_pulse, pool, place, pick, eye]


def turned_quarter(re, im, sign):
    return (im, -re) if sign < 0 else (-im, re)


def dft4(x, sign):
    (r0, i0), (r1, i1), (r2, i2), (r3, i3) = x
    sr0, si0, dr0, di0 = r0 + r2, i0 + i2, r0 - r2, i0 - i2
    sr1, si1, dr1, di1 = r1 + r3, i1 + i3, r1 - r3, i1 - i3
    tr, ti = turned_quarter(dr1, di1, sign)
    return [(sr0 + sr1, si0 + si1), (dr0 + tr, di0 + ti), (sr0 - sr1, si0 - si1), (dr0 - tr, di0 - ti)]


def dft16(x, sign):
    stage = []
    for n2 in range(4):
        part = dft4([x[4 * n1 + n2] for n1 in range(4)], sign)
        moved = []
        for k1 in range(4):
            re, im = part[k1]
            if n2 * k1:
                angle = sign * 2.0 * math.pi * n2 * k1 / 16
                c, s = math.cos(angle), math.sin(angle)
                if n2 * k1 == 4:
                    re, im = turned_quarter(re, im, sign)
                else:
                    re, im = re * c - im * s, re * s + im * c
            moved.append((re, im))
        stage.append(moved)
    out = [None] * 16
    for k1 in range(4):
        last = dft4([stage[n2][k1] for n2 in range(4)], sign)
        for k2 in range(4):
            out[k1 + 4 * k2] = last[k2]
    return out


def swapped(v):
    return pltpu.roll(v, 64, 1)


def packed_dft4(x, unit):
    s0, d0, s1, d1 = x[0] + x[2], x[0] - x[2], x[1] + x[3], x[1] - x[3]
    t = swapped(d1) * unit
    return [s0 + s1, d0 + t, s0 - s1, d0 - t]


def packed_dft16(x, sign, unit):
    stage = []
    for n2 in range(4):
        part = packed_dft4([x[4 * n1 + n2] for n1 in range(4)], unit)
        moved = []
        for k1 in range(4):
            v = part[k1]
            if n2 * k1:
                angle = 2.0 * math.pi * n2 * k1 / 16
                c, s = math.cos(angle), math.sin(angle)
                v = swapped(v) * unit if n2 * k1 == 4 else v * c + swapped(v) * (unit * s)
            moved.append(v)
        stage.append(moved)
    out = [None] * 16
    for k1 in range(4):
        last = packed_dft4([stage[n2][k1] for n2 in range(4)], unit)
        for k2 in range(4):
            out[k1 + 4 * k2] = last[k2]
    return out


def halves(x):
    high = x.astype(jnp.bfloat16)
    return high, (x - high.astype(F32)).astype(jnp.bfloat16)


def dot(x, w, precision=None):
    return lax.dot_general(x, w, (((1,), (0,)), ((), ())), precision=precision, preferred_element_type=F32)


def dot_wide(x, w):
    high, low = halves(x)
    return dot(jnp.concatenate([high, low, high], axis=1), w)


def dot_square(x, w):
    y = dot(jnp.concatenate(halves(x), axis=1), w)
    return y[:, 0:128] + y[:, 128:256]


def dot_nt(x, w, precision=EXACT):
    return lax.dot_general(x, w, (((1,), (1,)), ((), ())), precision=precision, preferred_element_type=F32)


def kernel(
    raw, rfil, afil, inv, mask,
    w1_h, w2_h, tr_h, w3_h, w4_h, tp_h, pool_h, place_h, pick_h, eye_h,
    out,
    x, rf, af, iv, w1, w2, tr, w3, w4, tp, pool, place, pick, eye,
    spec, gain, turned, sent, got, mid, fcos, fsin, scene, stack, prod, look,
    wmine, wall, wide, side_s, side_r, low_s, low_r, slope, part_s, part_r,
    ld, ldx, s1, r1, s2, r2, s3, r3, s4, r4, s5, r5,
):
    a, s = lax.axis_index("acq"), lax.axis_index("strip")

    def load_x(g):
        rows = pl.ds(pl.multiple_of(8 * g, 8), 8)
        return pltpu.make_async_copy(raw.at[0, :, rows, :], x.at[:, rows, :], ldx.at[g])

    loads = [
        pltpu.make_async_copy(src, dst, ld.at[i])
        for i, (src, dst) in enumerate([
            (tr_h, tr), (rfil, rf), (inv, iv), (place_h, place), (eye_h, eye), (w1_h, w1), (w2_h, w2),
            (w3_h, w3), (w4_h, w4), (tp_h, tp), (pick_h, pick), (pool_h, pool), (afil, af),
        ])
    ]
    for copy in loads[:3]:
        copy.start()
    for g in range(8):
        load_x(g).start()
    for copy in loads[3:]:
        copy.start()

    barrier = pltpu.get_barrier_semaphore()

    def greet(i, _):
        pl.semaphore_signal(barrier, inc=1, device_id=(a, lax.rem(s + i, DEV)), device_id_type=MESH)
        pl.semaphore_signal(barrier, inc=1, device_id=(lax.rem(a + i, DEV), s), device_id_type=MESH)
        return 0

    lax.fori_loop(1, DEV, greet, 0)

    lane = lax.broadcasted_iota(jnp.int32, (8, LANES), 1)
    row8 = lax.broadcasted_iota(jnp.int32, (8, LANES), 0)
    half = jnp.where(lane < 64, -1.0, 1.0).astype(F32)

    loads[0].wait()
    loads[1].wait()
    loads[2].wait()
    usable = [jnp.where(a >= l + 1, mask[0, l].astype(F32), 0.0) for l in range(2)]
    wmine[...] = jnp.zeros((8, LANES), F32)
    for l in range(2):
        wmine[pl.ds(l, 1), pl.ds(0, DEV)] = iv[pl.ds(l, 1), :] * usable[l]

    def forward_range(g, _):
        load_x(g).wait()
        rows = pl.ds(pl.multiple_of(8 * g, 8), 8)
        field = [(x[0, rows, pl.ds(128 * n, 128)], x[1, rows, pl.ds(128 * n, 128)]) for n in range(16)]
        for k, (re, im) in enumerate(dft16(field, -1.0)):
            c, t = tr[pl.ds(k, 1), :], tr[pl.ds(16 + k, 1), :]
            at = pl.ds(pl.multiple_of(64 * k + 8 * g, 8), 8)
            spec[at, pl.ds(0, 128)] = re * c - im * t
            spec[at, pl.ds(128, 128)] = re * t + im * c
        return 0

    lax.fori_loop(0, 8, forward_range, 0)

    for copy in loads[3:5]:
        copy.wait()
    for c in range(2):
        for k in range(16):
            gain[pl.ds(16 * c + k, 1), pl.ds(0, 128)] = rf[pl.ds(c, 1), pl.ds(128 * k, 128)]
    across = dot_nt(eye[...], gain[:, pl.ds(0, 128)])
    ordered = dot(across[0:16, :], place[pl.ds(0, 32), :], EXACT)
    for m in range(1, 8):
        ordered = ordered + dot(across[16 * m : 16 * m + 16, :], place[pl.ds(32 * m, 32), :], EXACT)
    gain[pl.ds(0, 16), :] = ordered

    for copy in loads[5:7]:
        copy.wait()

    def filter_range(k, _):
        rows = pl.ds(pl.multiple_of(256 * k, 256), 256)
        z = dot_wide(spec[rows, :], w1[...])
        parts = []
        for i in range(4):
            g = gain[pl.ds(4 * k + i, 1), :]
            re, im = z[64 * i : 64 * i + 64, 0:128], z[64 * i : 64 * i + 64, 128:256]
            gr, gi = g[:, 0:128], g[:, 128:256]
            parts.append(jnp.concatenate([re * gr - im * gi, re * gi + im * gr], axis=1))
        y = dot_wide(jnp.concatenate(parts, axis=0), w2[...])
        for i in range(4):
            c, t = tr[pl.ds(32 + 4 * k + i, 1), :], tr[pl.ds(48 + 4 * k + i, 1), :]
            re, im = y[64 * i : 64 * i + 64, 0:128], y[64 * i : 64 * i + 64, 128:256]
            at = pl.ds(pl.multiple_of(256 * k + 64 * i, 64), 64)
            spec[at, pl.ds(0, 128)] = re * c - im * t
            spec[at, pl.ds(128, 128)] = re * t + im * c
        return 0

    lax.fori_loop(0, 4, filter_range, 0)

    def inverse_range(g, _):
        field = []
        for k in range(16):
            at = pl.ds(pl.multiple_of(64 * k + 8 * g, 8), 8)
            field.append((spec[at, pl.ds(0, 128)], spec[at, pl.ds(128, 128)]))
        for n, (re, im) in enumerate(dft16(field, 1.0)):
            turned[pl.ds(pl.multiple_of(128 * n + 8 * g, 8), 8), :] = re
            turned[pl.ds(pl.multiple_of(128 * n + 64 + 8 * g, 8), 8), :] = im
        return 0

    lax.fori_loop(0, 8, inverse_range, 0)

    pl.semaphore_wait(barrier, 2 * (DEV - 1))

    def strip_copy(h, i):
        p = lax.rem(s + i, DEV)
        return pltpu.make_async_remote_copy(
            src_ref=sent.at[pl.ds(pl.multiple_of(128 * p + WIDE * h, WIDE), WIDE), :],
            dst_ref=got.at[pl.ds(pl.multiple_of(128 * s + WIDE * h, WIDE), WIDE), :],
            send_sem=s1.at[h, i], recv_sem=r1.at[h, i], device_id=(a, p), device_id_type=MESH,
        )

    def acq_copy(h, i):
        p = lax.rem(a + i, DEV)
        return pltpu.make_async_remote_copy(
            src_ref=scene.at[pl.ds(pl.multiple_of(128 * p + WIDE * h, WIDE), WIDE), :],
            dst_ref=stack.at[pl.ds(pl.multiple_of(128 * a + WIDE * h, WIDE), WIDE), :],
            send_sem=s2.at[h, i], recv_sem=r2.at[h, i], device_id=(p, s), device_id_type=MESH,
        )

    def weight_copy(i):
        p = lax.rem(a + i, DEV)
        return pltpu.make_async_remote_copy(
            src_ref=wmine, dst_ref=wall.at[pl.ds(pl.multiple_of(8 * a, 8), 8), :],
            send_sem=s3.at[i], recv_sem=r3.at[i], device_id=(p, s), device_id_type=MESH,
        )

    def part_copy(i):
        p = lax.rem(a + i, DEV)
        return pltpu.make_async_remote_copy(
            src_ref=part_s.at[pl.ds(pl.multiple_of(8 * p, 8), 8), :],
            dst_ref=part_r.at[pl.ds(pl.multiple_of(8 * a, 8), 8), :],
            send_sem=s4.at[i], recv_sem=r4.at[i], device_id=(p, s), device_id_type=MESH,
        )

    def first_send(i, _):
        p = lax.rem(s + i, DEV)
        at = pl.ds(pl.multiple_of(128 * p, 128), 128)
        sent[at, :] = turned[at, :].T
        strip_copy(0, i).start()
        return 0

    lax.fori_loop(1, DEV, first_send, 0)
    for h in range(1, CHUNKS):
        lax.fori_loop(1, DEV, lambda i, _, h=h: (strip_copy(h, i).start(), 0)[1], 0)
    lax.fori_loop(1, DEV, lambda i, _: (weight_copy(i).start(), 0)[1], 0)
    own = pl.ds(pl.multiple_of(128 * s, 128), 128)
    got[own, :] = turned[own, :].T
    wall[pl.ds(pl.multiple_of(8 * a, 8), 8), :] = wmine[...]

    for copy in loads[7:]:
        copy.wait()

    def turn_filter(k, _):
        re, im = af[0, pl.ds(k, 64, stride=16), :], af[1, pl.ds(k, 64, stride=16), :]
        c = dot_nt(pick[...], jnp.concatenate([re, re], axis=0))
        t = dot_nt(pick[...], jnp.concatenate([-im, im], axis=0))
        for h in range(CHUNKS):
            at = pl.ds(pl.multiple_of(512 * h + WIDE * k, WIDE), WIDE)
            fcos[at, :] = c[WIDE * h : WIDE * h + WIDE, :]
            fsin[at, :] = t[WIDE * h : WIDE * h + WIDE, :]
        return 0

    lax.fori_loop(0, 16, turn_filter, 0)

    lax.fori_loop(1, DEV, lambda i, _: (weight_copy(i).wait_recv(), 0)[1], 0)
    for l in range(2):
        columns = wall[pl.ds(l, 16, stride=8), :]
        for e in range(DEV):
            wide[pl.ds(16 * (16 * l + e), 16), :] = jnp.broadcast_to(columns[:, e : e + 1], (16, LANES))

    def azimuth(h):
        def forward(m, _):
            field = [got[pl.ds(pl.multiple_of(128 * n + WIDE * h + 8 * m, 8), 8), :] for n in range(16)]
            for k, v in enumerate(packed_dft16(field, -1.0, -half)):
                v = v * tp[pl.ds(k, 1), :] + swapped(v) * tp[pl.ds(16 + k, 1), :]
                mid[pl.ds(pl.multiple_of(WIDE * k + 8 * m, 8), 8), :] = v
            return 0

        lax.fori_loop(0, 4, forward, 0)
        at = pl.ds(pl.multiple_of(512 * h, 512), 512)
        z = dot_square(mid[...], w3[...])
        z = z * fcos[at, :] + swapped(z) * fsin[at, :]
        z = dot_square(z, w4[...])
        z2 = swapped(z)
        for k in range(16):
            piece = slice(WIDE * k, WIDE * k + WIDE)
            mid[pl.ds(WIDE * k, WIDE), :] = (
                z[piece, :] * tp[pl.ds(32 + k, 1), :] + z2[piece, :] * tp[pl.ds(48 + k, 1), :]
            )

        def inverse(m, _):
            field = [mid[pl.ds(pl.multiple_of(WIDE * k + 8 * m, 8), 8), :] for k in range(16)]
            for n, v in enumerate(packed_dft16(field, 1.0, half)):
                scene[pl.ds(pl.multiple_of(128 * n + WIDE * h + 8 * m, 8), 8), :] = v
            return 0

        lax.fori_loop(0, 4, inverse, 0)

    def products(h):
        held = {}
        for j in range(DEV):
            held[j] = [stack[pl.ds(pl.multiple_of(128 * j + WIDE * h + 8 * m, 8), 8), :] for m in range(4)]
            later = [swapped(v) for v in held[j]]
            for l in (1, 2):
                if j >= l:
                    same, cross = 0.0, 0.0
                    for m in range(4):
                        same = same + held[j - l][m] * held[j][m]
                        cross = cross + held[j - l][m] * later[m]
                    p = PAIRS.index((l, j))
                    prod[pl.ds(8 * p, 8), pl.ds(0, 128)] = same
                    prod[pl.ds(8 * p, 8), pl.ds(128, 128)] = cross
        pooled = dot(jnp.concatenate(halves(prod[...]), axis=1), pool[pl.ds(pl.multiple_of(512 * h, 512), 512), :])

        @pl.when(h == 0)
        def _():
            look[...] = pooled

        @pl.when(h > 0)
        def _():
            look[...] += pooled

    def turn(h, _):
        @pl.when(h < CHUNKS)
        def _():
            lax.fori_loop(1, DEV, lambda i, _: (strip_copy(h, i).wait_recv(), 0)[1], 0)
            azimuth(h)
            lax.fori_loop(1, DEV, lambda i, _: (acq_copy(h, i).start(), 0)[1], 0)
            stack[pl.ds(pl.multiple_of(128 * a + WIDE * h, WIDE), WIDE), :] = scene[
                pl.ds(pl.multiple_of(128 * a + WIDE * h, WIDE), WIDE), :
            ]

        @pl.when(h > 0)
        def _():
            lax.fori_loop(1, DEV, lambda i, _: (acq_copy(h - 1, i).wait_recv(), 0)[1], 0)
            products(h - 1)

        return 0

    lax.fori_loop(0, CHUNKS + 1, turn, 0)

    side = [jnp.zeros((8, LANES), F32), jnp.zeros((8, LANES), F32)]
    for p in range(len(PAIRS)):
        v = look[pl.ds(8 * p, 8), :]
        v = pltpu.roll(v, p % 16, 1) if p % 16 else v
        side[p // 16] = jnp.where(lane % 16 == p % 16, v, side[p // 16])
    side_s[pl.ds(0, 8), :] = side[0]
    side_s[pl.ds(8, 8), :] = side[1]
    low_s[pl.ds(0, len(PAIRS)), :] = look[pl.ds(0, len(PAIRS), stride=8), :]
    side_copy = pltpu.make_async_remote_copy(
        src_ref=side_s, dst_ref=side_r, send_sem=s5.at[0], recv_sem=r5.at[0],
        device_id=(lax.rem(a + DEV - 1, DEV), s), device_id_type=MESH,
    )
    low_copy = pltpu.make_async_remote_copy(
        src_ref=low_s.at[pl.ds(0, len(PAIRS)), :], dst_ref=low_r.at[pl.ds(0, len(PAIRS)), :], send_sem=s5.at[1], recv_sem=r5.at[1],
        device_id=(a, lax.rem(s + DEV - 1, DEV)), device_id_type=MESH,
    )
    side_copy.start()
    low_copy.start()
    side_copy.wait_recv()
    low_copy.wait_recv()

    inner = a < DEV - 1
    above = s < DEV - 1
    border = [jnp.where(inner, side_r[pl.ds(8 * i, 8), :], 0.0) for i in range(2)]
    low_r[...] = jnp.where(above, pltpu.roll(low_r[...], 112, 1), 0.0)
    last_look = lane % 16 == 15
    corner = (row8 == 7) & (lane % 64 >= 48)
    for p in range(len(PAIRS)):
        v = look[pl.ds(8 * p, 8), :]
        after = pltpu.roll(v, 63, 1)
        edge = pltpu.roll(border[p // 16], (64 + 15 - p % 16) % 128, 1)
        after = jnp.where(last_look, edge, after)
        up = jnp.where(row8 == 0, pltpu.roll(v, 48, 1), pltpu.roll(v, 64, 1))
        up = pltpu.roll(up, 7, 0)
        up = jnp.where(corner, jnp.broadcast_to(low_r[pl.ds(p, 1), :], (8, LANES)), up)
        w = v * -half
        azim, rang = w * after, w * up
        slope[pl.ds(8 * p, 8), :] = jnp.where(lane < 64, azim, rang) + pltpu.roll(
            jnp.where(lane < 64, rang, azim), 64, 1
        )

    total = [None] * DEV
    for p, (l, j) in enumerate(PAIRS):
        v = slope[pl.ds(8 * p, 8), :]
        for e in range(DEV):
            term = wide[pl.ds(16 * (16 * (l - 1) + e) + j, 1), :] * v
            total[e] = term if total[e] is None else total[e] + term
    for e in range(DEV):
        part_s[pl.ds(8 * e, 8), :] = total[e]
    lax.fori_loop(1, DEV, lambda i, _: (part_copy(i).start(), 0)[1], 0)
    mine = pl.ds(pl.multiple_of(8 * a, 8), 8)
    part_r[mine, :] = part_s[mine, :]
    lax.fori_loop(1, DEV, lambda i, _: (part_copy(i).wait_recv(), 0)[1], 0)

    for d in range(2):
        for h in range(CHUNKS):
            for u in range(2):
                tile = None
                for t in range(8):
                    v = part_r[pl.ds(8 * (8 * u + t), 8), :]
                    shift = 16 * (t - 4 * d - h) % 128
                    v = pltpu.roll(v, shift, 1) if shift else v
                    tile = v if tile is None else jnp.where(lane // 16 == t, v, tile)
                out[0, d, pl.ds(8 * h, 8), pl.ds(128 * u, 128)] = tile

    for h in range(CHUNKS):
        lax.fori_loop(1, DEV, lambda i, _, h=h: (strip_copy(h, i).wait_send(), 0)[1], 0)
        lax.fori_loop(1, DEV, lambda i, _, h=h: (acq_copy(h, i).wait_send(), 0)[1], 0)
    lax.fori_loop(1, DEV, lambda i, _: (weight_copy(i).wait_send(), 0)[1], 0)
    lax.fori_loop(1, DEV, lambda i, _: (part_copy(i).wait_send(), 0)[1], 0)
    side_copy.wait_send()
    low_copy.wait_send()


def per_device(raw_echoes, range_filter, azimuth_filter, pair_mask, inversion):
    consts = tables()
    hbm = pl.BlockSpec(memory_space=pl.ANY)
    smem = pl.BlockSpec(memory_space=pltpu.SMEM)
    vmem = lambda *shape: pltpu.VMEM(shape, F32)
    dma = pltpu.SemaphoreType.DMA
    return pl.pallas_call(
        kernel,
        out_shape=jax.ShapeDtypeStruct((1, 2, WIDE, 256), F32),
        in_specs=[hbm, hbm, hbm, hbm, smem] + [hbm] * len(consts),
        out_specs=pl.BlockSpec(memory_space=pltpu.VMEM),
        scratch_shapes=[vmem(2, 64, 2048), vmem(2, 2048), vmem(2, 1024, 128), vmem(2, DEV)]
        + [pltpu.VMEM(c.shape, c.dtype) for c in consts]
        + [
            vmem(1024, 256), vmem(32, 256), vmem(2048, 128), vmem(2048, 128), vmem(2048, 128),
            vmem(512, 128), vmem(2048, 128), vmem(2048, 128), vmem(2048, 128), vmem(2048, 128),
            vmem(ROWS, 256), vmem(ROWS, 128),
            vmem(8, 128), vmem(128, 128), vmem(512, 128), vmem(16, 128), vmem(16, 128), vmem(32, 128), vmem(32, 128),
            vmem(ROWS, 128), vmem(128, 128), vmem(128, 128),
            dma((13,)), dma((8,)), dma((CHUNKS, DEV)), dma((CHUNKS, DEV)), dma((CHUNKS, DEV)), dma((CHUNKS, DEV)),
            dma((DEV,)), dma((DEV,)), dma((DEV,)), dma((DEV,)), dma((2,)), dma((2,)),
        ],
        compiler_params=pltpu.CompilerParams(collective_id=0, has_side_effects=True, vmem_limit_bytes=60 * 1024 * 1024),
    )(raw_echoes, range_filter, azimuth_filter, inversion[:, 0, :].T, pair_mask, *[jnp.asarray(c) for c in consts])


def solution(mesh):
    return jax.shard_map(
        per_device,
        mesh=mesh,
        in_specs=(
            P("acq", None, "strip", None),
            P(),
            P(None, None, "strip"),
            P("acq", None),
            P(None, "acq", None),
        ),
        out_specs=P("acq", None, "strip", None),
        check_vma=False,
    )
```

```python
import functools
import math

import jax
import jax.numpy as jnp
import numpy as np
from jax import lax
from jax.experimental import pallas as pl
from jax.experimental.pallas import tpu as pltpu
from jax.sharding import PartitionSpec as P

MESH = pl.DeviceIdType.MESH
EXACT = lax.Precision.HIGHEST
F32 = jnp.float32
LANES = 128
DEV = 16
Q = 64
CHUNKS = 4
WIDE = 32
TILES = 16
PAIR_UNITS = 7
LAG = 3
UNITS = [(2 * u, 2) for u in range(PAIR_UNITS)] + [(t, 1) for t in range(2 * PAIR_UNITS, TILES)]
PAIRS = [(1, j) for j in range(1, DEV)] + [(2, j) for j in range(2, DEV)]
ROWS = 8 * len(PAIRS)


def block_table(size, sign, scale=1.0):
    index = np.arange(size)
    angle = sign * 2.0 * math.pi / size * (index[:, None] * index[None, :] % size)
    cosine, sine = np.cos(angle) * scale, np.sin(angle) * scale
    return np.block([[cosine, sine], [-sine, cosine]])


def turn_table(count, width, size, sign):
    angle = sign * 2.0 * math.pi / size * (np.arange(count)[:, None] * np.arange(width)[None, :] % size)
    return np.cos(angle), np.sin(angle)


def sample_order():
    order = np.zeros(LANES, dtype=np.int64)
    for h in range(CHUNKS):
        for m in range(4):
            for k in range(8):
                order[WIDE * h + 8 * m + k] = WIDE * h + 4 * k + m
    return order


def tables():
    order = sample_order()
    w1 = block_table(128, -1.0)
    w2 = block_table(128, 1.0, 1.0 / 2048)
    w2 = w2[:, np.concatenate([order, 128 + order])]
    c1, s1 = turn_table(16, 128, 2048, -1.0)
    c2, s2 = turn_table(16, 128, 2048, 1.0)
    turn_range = np.concatenate([c1, s1, c2[:, order], s2[:, order]])
    w3 = block_table(64, -1.0)
    w4 = block_table(64, 1.0, 1.0 / 1024)
    c3, s3 = turn_table(16, 64, 1024, -1.0)
    c4, s4 = turn_table(16, 64, 1024, 1.0)
    turn_pulse = np.concatenate(
        [np.hstack([c3, c3]), np.hstack([-s3, s3]), np.hstack([c4, c4]), np.hstack([-s4, s4])]
    )
    pool = np.zeros((CHUNKS, 256, LANES))
    for h in range(CHUNKS):
        for q in range(Q):
            real, imag = 16 * h + q // 4, 64 + 16 * h + q // 4
            pool[h, q, real] = 0.25
            pool[h, 64 + q, real] = 0.25
            pool[h, 128 + q, imag] = -0.25
            pool[h, 192 + q, imag] = 0.25
    pick = np.zeros((LANES, LANES))
    pick[np.arange(LANES), order] = 1.0
    def split(w):
        high = np.asarray(w, np.float32).astype(jnp.bfloat16)
        return high, (w - high.astype(np.float64)).astype(np.float32).astype(jnp.bfloat16)

    def stacked(w):
        high, low = split(w)
        return np.concatenate([high, high, low])

    def squared(w):
        both = np.concatenate(split(w), axis=1)
        return np.concatenate([both, both])

    pool = np.concatenate([pool, pool], axis=1).reshape(-1, LANES).astype(jnp.bfloat16)
    turn_range, turn_pulse = np.asarray(turn_range, np.float32), np.asarray(turn_pulse, np.float32)
    pick = np.concatenate([pick, pick, pick], axis=1).astype(jnp.bfloat16)
    return [stacked(w1), stacked(w2), turn_range, squared(w3), squared(w4), turn_pulse, pool, pick]


def turned_quarter(re, im, sign):
    return (im, -re) if sign < 0 else (-im, re)


def dft4(x, sign):
    (r0, i0), (r1, i1), (r2, i2), (r3, i3) = x
    sr0, si0, dr0, di0 = r0 + r2, i0 + i2, r0 - r2, i0 - i2
    sr1, si1, dr1, di1 = r1 + r3, i1 + i3, r1 - r3, i1 - i3
    tr, ti = turned_quarter(dr1, di1, sign)
    return [(sr0 + sr1, si0 + si1), (dr0 + tr, di0 + ti), (sr0 - sr1, si0 - si1), (dr0 - tr, di0 - ti)]


def dft16(x, sign):
    stage = []
    for n2 in range(4):
        part = dft4([x[4 * n1 + n2] for n1 in range(4)], sign)
        moved = []
        for k1 in range(4):
            re, im = part[k1]
            if n2 * k1:
                angle = sign * 2.0 * math.pi * n2 * k1 / 16
                c, s = math.cos(angle), math.sin(angle)
                if n2 * k1 == 4:
                    re, im = turned_quarter(re, im, sign)
                else:
                    re, im = re * c - im * s, re * s + im * c
            moved.append((re, im))
        stage.append(moved)
    out = [None] * 16
    for k1 in range(4):
        last = dft4([stage[n2][k1] for n2 in range(4)], sign)
        for k2 in range(4):
            out[k1 + 4 * k2] = last[k2]
    return out


def swapped(v):
    return pltpu.roll(v, 64, 1)


def packed_dft4(x, unit):
    s0, d0, s1, d1 = x[0] + x[2], x[0] - x[2], x[1] + x[3], x[1] - x[3]
    t = swapped(d1) * unit
    return [s0 + s1, d0 + t, s0 - s1, d0 - t]


def packed_dft16(x, sign, unit):
    stage = []
    for n2 in range(4):
        part = packed_dft4([x[4 * n1 + n2] for n1 in range(4)], unit)
        moved = []
        for k1 in range(4):
            v = part[k1]
            if n2 * k1:
                angle = 2.0 * math.pi * n2 * k1 / 16
                c, s = math.cos(angle), math.sin(angle)
                v = swapped(v) * unit if n2 * k1 == 4 else v * c + swapped(v) * (unit * s)
            moved.append(v)
        stage.append(moved)
    out = [None] * 16
    for k1 in range(4):
        last = packed_dft4([stage[n2][k1] for n2 in range(4)], unit)
        for k2 in range(4):
            out[k1 + 4 * k2] = last[k2]
    return out


def halves(x):
    high = x.astype(jnp.bfloat16)
    return high, (x - high.astype(F32)).astype(jnp.bfloat16)


def dot(x, w, precision=None):
    return lax.dot_general(x, w, (((1,), (0,)), ((), ())), precision=precision, preferred_element_type=F32)


def dot_wide(x, w):
    high, low = halves(x)
    return dot(jnp.concatenate([high, low, high], axis=1), w)


def dot_square(x, w):
    y = dot(jnp.concatenate(halves(x), axis=1), w)
    return y[:, 0:128] + y[:, 128:256]


def dot_nt(x, w, precision=EXACT):
    return lax.dot_general(x, w, (((1,), (1,)), ((), ())), precision=precision, preferred_element_type=F32)


def kernel(
    raw, rfil, afil, inv, mask,
    w1_h, w2_h, tr_h, w3_h, w4_h, tp_h, pool_h, pick_h,
    out,
    x, rf, af, iv, w1, w2, tr, w3, w4, tp, pool, pick,
    spec, gain, turned, sent, got, mid, fcos, fsin, scene, stack, prod, look,
    wmine, wall, wide, side_s, side_r, low_s, low_r, slope, part_s, part_r,
    ld, ldx, s1, r1, s2, r2, s3, r3,
):
    a, s = lax.axis_index("acq"), lax.axis_index("strip")

    barrier = pltpu.get_barrier_semaphore()

    def greet(i, _):
        pl.semaphore_signal(barrier, inc=1, device_id=(a, lax.rem(s + i, DEV)), device_id_type=MESH)
        pl.semaphore_signal(barrier, inc=1, device_id=(lax.rem(a + i, DEV), s), device_id_type=MESH)
        return 0

    lax.fori_loop(1, DEV, greet, 0, unroll=True)

    def load_x(g):
        rows = pl.ds(pl.multiple_of(8 * g, 8), 8)
        return pltpu.make_async_copy(raw.at[0, :, rows, :], x.at[:, rows, :], ldx.at[g])

    loads = [
        pltpu.make_async_copy(src, dst, ld.at[i])
        for i, (src, dst) in enumerate([
            (rfil, rf), (inv, iv), (tr_h, tr), (w1_h, w1), (w2_h, w2),
            (pick_h, pick), (afil, af), (w3_h, w3), (w4_h, w4), (tp_h, tp), (pool_h, pool),
        ])
    ]
    for copy in loads[:3]:
        copy.start()
    for g in range(8):
        load_x(g).start()
    for copy in loads[3:]:
        copy.start()

    lane = lax.broadcasted_iota(jnp.int32, (8, LANES), 1)
    row8 = lax.broadcasted_iota(jnp.int32, (8, LANES), 0)
    half = jnp.where(lane < 64, -1.0, 1.0).astype(F32)

    loads[0].wait()
    loads[1].wait()
    usable = [jnp.where(a >= l + 1, mask[0, l].astype(F32), 0.0) for l in range(2)]
    wmine[...] = jnp.zeros((8, LANES), F32)
    for l in range(2):
        wmine[pl.ds(l, 1), pl.ds(0, DEV)] = iv[pl.ds(l, 1), :] * usable[l]

    for c in range(2):
        for k in range(16):
            gain[pl.ds(16 * c + k, 1), pl.ds(0, 128)] = rf[pl.ds(c, 1), pl.ds(128 * k, 128)]
    eye = (lax.broadcasted_iota(jnp.int32, (128, 128), 0) == lax.broadcasted_iota(jnp.int32, (128, 128), 1)).astype(F32)
    across = dot_nt(eye, gain[:, pl.ds(0, 128)])
    to = lax.broadcasted_iota(jnp.int32, (32, 256), 1)
    meets = to // 8 == lax.broadcasted_iota(jnp.int32, (32, 256), 0)
    ordered = None
    for m in range(8):
        place = jnp.where(meets & (to % 8 == m), 1.0, 0.0).astype(F32)
        part = dot(across[16 * m : 16 * m + 16, :], place, EXACT)
        ordered = part if ordered is None else ordered + part
    gain[pl.ds(0, 16), :] = ordered
    loads[2].wait()

    def forward_range(g, _):
        load_x(g).wait()
        rows = pl.ds(pl.multiple_of(8 * g, 8), 8)
        field = [(x[0, rows, pl.ds(128 * n, 128)], x[1, rows, pl.ds(128 * n, 128)]) for n in range(16)]
        for k, (re, im) in enumerate(dft16(field, -1.0)):
            c, t = tr[pl.ds(k, 1), :], tr[pl.ds(16 + k, 1), :]
            at = pl.ds(pl.multiple_of(64 * k + 8 * g, 8), 8)
            spec[at, pl.ds(0, 128)] = re * c - im * t
            spec[at, pl.ds(128, 128)] = re * t + im * c
        return 0

    lax.fori_loop(0, 8, forward_range, 0, unroll=2)

    for copy in loads[3:5]:
        copy.wait()

    def filter_range(k, _):
        rows = pl.ds(pl.multiple_of(256 * k, 256), 256)
        z = dot_wide(spec[rows, :], w1[...])
        parts = []
        for i in range(4):
            g = gain[pl.ds(4 * k + i, 1), :]
            re, im = z[64 * i : 64 * i + 64, 0:128], z[64 * i : 64 * i + 64, 128:256]
            gr, gi = g[:, 0:128], g[:, 128:256]
            parts.append(jnp.concatenate([re * gr - im * gi, re * gi + im * gr], axis=1))
        y = dot_wide(jnp.concatenate(parts, axis=0), w2[...])
        for i in range(4):
            c, t = tr[pl.ds(32 + 4 * k + i, 1), :], tr[pl.ds(48 + 4 * k + i, 1), :]
            re, im = y[64 * i : 64 * i + 64, 0:128], y[64 * i : 64 * i + 64, 128:256]
            at = pl.ds(pl.multiple_of(256 * k + 64 * i, 64), 64)
            spec[at, pl.ds(0, 128)] = re * c - im * t
            spec[at, pl.ds(128, 128)] = re * t + im * c
        return 0

    lax.fori_loop(0, 4, filter_range, 0, unroll=True)

    def inverse_range(g, _):
        field = []
        for k in range(16):
            at = pl.ds(pl.multiple_of(64 * k + 8 * g, 8), 8)
            field.append((spec[at, pl.ds(0, 128)], spec[at, pl.ds(128, 128)]))
        for n, (re, im) in enumerate(dft16(field, 1.0)):
            turned[pl.ds(pl.multiple_of(128 * n + 8 * g, 8), 8), :] = re
            turned[pl.ds(pl.multiple_of(128 * n + 64 + 8 * g, 8), 8), :] = im
        return 0

    lax.fori_loop(0, 8, inverse_range, 0, unroll=2)

    def rows_of(block, tile, count):
        return pl.ds(pl.multiple_of(128 * block + 8 * tile, 8), 8 * count)

    def strip_copy(u, tile, count, i):
        p = lax.rem(s + i, DEV)
        return pltpu.make_async_remote_copy(
            src_ref=sent.at[rows_of(p, tile, count), :], dst_ref=got.at[rows_of(s, tile, count), :],
            send_sem=s1.at[0], recv_sem=r1.at[u], device_id=(a, p), device_id_type=MESH,
        )

    def acq_copy(u, tile, count, i):
        p = lax.rem(a + i, DEV)
        return pltpu.make_async_remote_copy(
            src_ref=scene.at[rows_of(p, tile, count), :], dst_ref=stack.at[rows_of(a, tile, count), :],
            send_sem=s2.at[0], recv_sem=r2.at[u], device_id=(p, s), device_id_type=MESH,
        )

    def weight_copy(i):
        p = lax.rem(a + i, DEV)
        return pltpu.make_async_remote_copy(
            src_ref=wmine, dst_ref=wall.at[pl.ds(pl.multiple_of(8 * a, 8), 8), :],
            send_sem=s3.at[0], recv_sem=r3.at[0], device_id=(p, s), device_id_type=MESH,
        )

    def part_copy(i):
        p = lax.rem(a + i, DEV)
        return pltpu.make_async_remote_copy(
            src_ref=part_s.at[pl.ds(pl.multiple_of(8 * p, 8), 8), :],
            dst_ref=part_r.at[pl.ds(pl.multiple_of(8 * a, 8), 8), :],
            send_sem=s3.at[1], recv_sem=r3.at[1], device_id=(p, s), device_id_type=MESH,
        )

    def wait_rows(ref, count, sem):
        rows = ref.at[pl.ds(0, 15 * count), :]
        pltpu.make_async_copy(rows, rows, sem).wait()

    def others(body):
        def step(i, _):
            body(i)
            return 0

        lax.fori_loop(1, DEV, step, 0)

    for n in range(16):
        sent[pl.ds(128 * n, 128), :] = turned[pl.ds(128 * n, 128), :].T
    pl.semaphore_wait(barrier, 2 * (DEV - 1))
    for u, (tile, count) in enumerate(UNITS):
        others(lambda i, u=u, tile=tile, count=count: strip_copy(u, tile, count, i).start())
    others(lambda i: weight_copy(i).start())
    own = pl.ds(pl.multiple_of(128 * s, 128), 128)
    got[own, :] = sent[own, :]
    wall[pl.ds(pl.multiple_of(8 * a, 8), 8), :] = wmine[...]

    for copy in loads[5:]:
        copy.wait()

    def turn_filter(k, _):
        re, im = af[0, pl.ds(k, 64, stride=16), :], af[1, pl.ds(k, 64, stride=16), :]
        both = jnp.concatenate([re, im], axis=0)
        b0 = both.astype(jnp.bfloat16)
        left = both - b0.astype(F32)
        b1 = left.astype(jnp.bfloat16)
        b2 = (left - b1.astype(F32)).astype(jnp.bfloat16)
        v = dot_nt(pick[...], jnp.concatenate([b0, b1, b2], axis=1), None)
        w = swapped(v)
        first = lax.broadcasted_iota(jnp.int32, (128, 128), 1) < 64
        c = jnp.where(first, v, w)
        t = jnp.where(first, -w, v)
        for q in range(TILES):
            at = pl.ds(pl.multiple_of(128 * q + 8 * k, 8), 8)
            fcos[at, :] = c[8 * q : 8 * q + 8, :]
            fsin[at, :] = t[8 * q : 8 * q + 8, :]
        return 0

    lax.fori_loop(0, 16, turn_filter, 0)

    wait_rows(wall, 8, r3.at[0])
    for l in range(2):
        columns = wall[pl.ds(l, 16, stride=8), :]
        for e in range(DEV):
            wide[pl.ds(16 * (16 * l + e), 16), :] = jnp.broadcast_to(columns[:, e : e + 1], (16, LANES))

    def azimuth(tile, count):
        for m in range(count):
            field = [got[rows_of(n, tile + m, 1), :] for n in range(16)]
            for k, v in enumerate(packed_dft16(field, -1.0, -half)):
                v = v * tp[pl.ds(k, 1), :] + swapped(v) * tp[pl.ds(16 + k, 1), :]
                mid[pl.ds(128 * m + 8 * k, 8), :] = v
        at = pl.ds(pl.multiple_of(128 * tile, 128), 128 * count)
        z = dot_square(mid[pl.ds(0, 128 * count), :], w3[...])
        z = z * fcos[at, :] + swapped(z) * fsin[at, :]
        z = dot_square(z, w4[...])
        z2 = swapped(z)
        for m in range(count):
            field = []
            for k in range(16):
                piece = slice(128 * m + 8 * k, 128 * m + 8 * k + 8)
                field.append(z[piece, :] * tp[pl.ds(32 + k, 1), :] + z2[piece, :] * tp[pl.ds(48 + k, 1), :])
            for n, v in enumerate(packed_dft16(field, 1.0, half)):
                scene[rows_of(n, tile + m, 1), :] = v

    def products(tile, count):
        held = {}
        for j in range(DEV):
            held[j] = [stack[rows_of(j, tile + m, 1), :] for m in range(count)]
            later = [swapped(v) for v in held[j]]
            for l in (1, 2):
                if j >= l:
                    same, cross = None, None
                    for m in range(count):
                        v, w = held[j - l][m] * held[j][m], held[j - l][m] * later[m]
                        same, cross = (v, w) if same is None else (same + v, cross + w)
                    p = PAIRS.index((l, j))
                    prod[pl.ds(8 * p, 8), pl.ds(0, 128)] = same
                    prod[pl.ds(8 * p, 8), pl.ds(128, 128)] = cross
        block = pl.ds(pl.multiple_of(512 * (tile // 4), 512), 512)
        pooled = dot(jnp.concatenate(halves(prod[...]), axis=1), pool[block, :])
        look[...] += pooled

    def focus(u, tile, count):
        wait_rows(got, 8 * count, r1.at[u])
        azimuth(tile, count)
        others(lambda i: acq_copy(u, tile, count, i).start())
        stack[rows_of(a, tile, count), :] = scene[rows_of(a, tile, count), :]

    def combine(u, tile, count):
        wait_rows(stack, 8 * count, r2.at[u])
        products(tile, count)

    look[...] = jnp.zeros_like(look)

    def turn(u, _):
        focus(u, 2 * u, 2)

        @pl.when(u >= LAG)
        def _():
            combine(u - LAG, 2 * (u - LAG), 2)

        return 0

    lax.fori_loop(0, PAIR_UNITS, turn, 0)

    low_s[...] = jnp.zeros_like(low_s)
    low_s[pl.ds(0, len(PAIRS)), :] = look[pl.ds(0, len(PAIRS), stride=8), :]
    low_copy = pltpu.make_async_remote_copy(
        src_ref=low_s, dst_ref=low_r, send_sem=s3.at[2], recv_sem=r3.at[2],
        device_id=(a, lax.rem(s + DEV - 1, DEV)), device_id_type=MESH,
    )

    @pl.when(s > 0)
    def _():
        low_copy.start()

    for u in range(PAIR_UNITS, len(UNITS)):
        focus(u, *UNITS[u])
    for u in range(PAIR_UNITS - LAG, len(UNITS)):
        combine(u, *UNITS[u])

    side = [jnp.zeros((8, LANES), F32), jnp.zeros((8, LANES), F32)]
    for p in range(len(PAIRS)):
        v = look[pl.ds(8 * p, 8), :]
        v = pltpu.roll(v, p % 16, 1) if p % 16 else v
        side[p // 16] = jnp.where(lane % 16 == p % 16, v, side[p // 16])
    side_s[pl.ds(0, 8), :] = side[0]
    side_s[pl.ds(8, 8), :] = side[1]
    side_copy = pltpu.make_async_remote_copy(
        src_ref=side_s, dst_ref=side_r, send_sem=s3.at[3], recv_sem=r3.at[3],
        device_id=(lax.rem(a + DEV - 1, DEV), s), device_id_type=MESH,
    )
    inner = a < DEV - 1
    above = s < DEV - 1

    @pl.when(a > 0)
    def _():
        side_copy.start()

    @pl.when(inner)
    def _():
        side_copy.wait_recv()

    @pl.when(above)
    def _():
        low_copy.wait_recv()

    border = [jnp.where(inner, side_r[pl.ds(8 * i, 8), :], 0.0) for i in range(2)]
    low_r[...] = jnp.where(above, pltpu.roll(low_r[...], 112, 1), 0.0)
    last_look = lane % 16 == 15
    corner = (row8 == 7) & (lane % 64 >= 48)
    for p in range(len(PAIRS)):
        v = look[pl.ds(8 * p, 8), :]
        after = pltpu.roll(v, 63, 1)
        edge = pltpu.roll(border[p // 16], (64 + 15 - p % 16) % 128, 1)
        after = jnp.where(last_look, edge, after)
        up = jnp.where(row8 == 0, pltpu.roll(v, 48, 1), pltpu.roll(v, 64, 1))
        up = pltpu.roll(up, 7, 0)
        up = jnp.where(corner, jnp.broadcast_to(low_r[pl.ds(p, 1), :], (8, LANES)), up)
        w = v * -half
        azim, rang = w * after, w * up
        slope[pl.ds(8 * p, 8), :] = jnp.where(lane < 64, azim, rang) + pltpu.roll(
            jnp.where(lane < 64, rang, azim), 64, 1
        )

    total = [None] * DEV
    for p, (l, j) in enumerate(PAIRS):
        v = slope[pl.ds(8 * p, 8), :]
        for e in range(DEV):
            term = wide[pl.ds(16 * (16 * (l - 1) + e) + j, 1), :] * v
            total[e] = term if total[e] is None else total[e] + term
    for e in range(DEV):
        part_s[pl.ds(8 * e, 8), :] = total[e]
    others(lambda i: part_copy(i).start())
    mine = pl.ds(pl.multiple_of(8 * a, 8), 8)
    part_r[mine, :] = part_s[mine, :]
    wait_rows(part_r, 8, r3.at[1])

    for d in range(2):
        for h in range(CHUNKS):
            for u in range(2):
                tile = None
                for t in range(8):
                    v = part_r[pl.ds(8 * (8 * u + t), 8), :]
                    shift = 16 * (t - 4 * d - h) % 128
                    v = pltpu.roll(v, shift, 1) if shift else v
                    tile = v if tile is None else jnp.where(lane // 16 == t, v, tile)
                out[0, d, pl.ds(8 * h, 8), pl.ds(128 * u, 128)] = tile

    wait_rows(sent, 128, s1.at[0])
    wait_rows(scene, 128, s2.at[0])
    wait_rows(wall, 8, s3.at[0])
    wait_rows(part_s, 8, s3.at[1])

    @pl.when(a > 0)
    def _():
        side_copy.wait_send()

    @pl.when(s > 0)
    def _():
        low_copy.wait_send()


def per_device(raw_echoes, range_filter, azimuth_filter, pair_mask, inversion):
    consts = tables()
    hbm = pl.BlockSpec(memory_space=pl.ANY)
    smem = pl.BlockSpec(memory_space=pltpu.SMEM)
    vmem = lambda *shape: pltpu.VMEM(shape, F32)
    dma = pltpu.SemaphoreType.DMA
    return pl.pallas_call(
        kernel,
        out_shape=jax.ShapeDtypeStruct((1, 2, WIDE, 256), F32),
        in_specs=[hbm, hbm, hbm, hbm, smem] + [hbm] * len(consts),
        out_specs=pl.BlockSpec(memory_space=pltpu.VMEM),
        scratch_shapes=[vmem(2, 64, 2048), vmem(2, 2048), vmem(2, 1024, 128), vmem(2, DEV)]
        + [pltpu.VMEM(c.shape, c.dtype) for c in consts]
        + [
            vmem(1024, 256), vmem(32, 256), vmem(2048, 128), vmem(2048, 128), vmem(2048, 128),
            vmem(256, 128), vmem(2048, 128), vmem(2048, 128), vmem(2048, 128), vmem(2048, 128),
            vmem(ROWS, 256), vmem(ROWS, 128),
            vmem(8, 128), vmem(128, 128), vmem(512, 128), vmem(16, 128), vmem(16, 128), vmem(32, 128), vmem(32, 128),
            vmem(ROWS, 128), vmem(128, 128), vmem(128, 128),
            dma((11,)), dma((8,)), dma((1,)), dma((len(UNITS),)), dma((1,)), dma((len(UNITS),)), dma((4,)), dma((4,)),
        ],
        compiler_params=pltpu.CompilerParams(collective_id=0, has_side_effects=True, vmem_limit_bytes=60 * 1024 * 1024),
    )(raw_echoes, range_filter, azimuth_filter, inversion[:, 0, :].T, pair_mask, *[jnp.asarray(c) for c in consts])


def solution(mesh):
    return jax.shard_map(
        per_device,
        mesh=mesh,
        in_specs=(
            P("acq", None, "strip", None),
            P(),
            P(None, None, "strip"),
            P("acq", None),
            P(None, "acq", None),
        ),
        out_specs=P("acq", None, "strip", None),
        check_vma=False,
    )
```

```python
import functools
import math

import jax
import jax.numpy as jnp
import numpy as np
from jax import lax
from jax.experimental import pallas as pl
from jax.experimental.pallas import tpu as pltpu
from jax.sharding import PartitionSpec as P

MESH = pl.DeviceIdType.MESH
EXACT = lax.Precision.HIGHEST
F32 = jnp.float32
LANES = 128
DEV = 16
ORDER = (8, 7, 9, 6, 10, 5, 11, 4, 12, 3, 13, 2, 14, 1, 15)
Q = 64
CHUNKS = 4
WIDE = 32
TILES = 16
LONG = 3
UNITS = [(4 * u, 4) for u in range(LONG)] + [(12, 2), (14, 1), (15, 1)]
PAIRS = [(1, j) for j in range(1, DEV)] + [(2, j) for j in range(2, DEV)]
ROWS = 8 * len(PAIRS)


def block_table(size, sign, scale=1.0):
    index = np.arange(size)
    angle = sign * 2.0 * math.pi / size * (index[:, None] * index[None, :] % size)
    cosine, sine = np.cos(angle) * scale, np.sin(angle) * scale
    return np.block([[cosine, sine], [-sine, cosine]])


def turn_table(count, width, size, sign):
    angle = sign * 2.0 * math.pi / size * (np.arange(count)[:, None] * np.arange(width)[None, :] % size)
    return np.cos(angle), np.sin(angle)


def sample_order():
    order = np.zeros(LANES, dtype=np.int64)
    for h in range(CHUNKS):
        for m in range(4):
            for k in range(8):
                order[WIDE * h + 8 * m + k] = WIDE * h + 4 * k + m
    return order


def tables():
    order = sample_order()
    w1 = block_table(128, -1.0)
    w2 = block_table(128, 1.0, 1.0 / 2048)
    w2 = w2[:, np.concatenate([order, 128 + order])]
    c1, s1 = turn_table(16, 128, 2048, -1.0)
    c2, s2 = turn_table(16, 128, 2048, 1.0)
    turn_range = np.concatenate([c1, s1, c2[:, order], s2[:, order]])
    w3 = block_table(64, -1.0)
    w4 = block_table(64, 1.0, 1.0 / 1024)
    c3, s3 = turn_table(16, 64, 1024, -1.0)
    c4, s4 = turn_table(16, 64, 1024, 1.0)
    turn_pulse = np.concatenate(
        [np.hstack([c3, c3]), np.hstack([-s3, s3]), np.hstack([c4, c4]), np.hstack([-s4, s4])]
    )
    pool = np.zeros((CHUNKS + 1, 256, LANES))
    for h in range(CHUNKS):
        for q in range(Q):
            real, imag = 16 * h + q // 4, 64 + 16 * h + q // 4
            pool[h, q, real] = 0.25
            pool[h, 64 + q, real] = 0.25
            pool[h, 128 + q, imag] = -0.25
            pool[h, 192 + q, imag] = 0.25
    for lane in range(LANES):
        at = 16 * (lane // 32) + 15
        pool[CHUNKS, lane, 64 + at] = 0.25
        pool[CHUNKS, 128 + lane, at] = -0.25 if lane % 8 < 4 else 0.25
    pick = np.zeros((LANES, LANES))
    pick[np.arange(LANES), order] = 1.0
    def split(w):
        high = np.asarray(w, np.float32).astype(jnp.bfloat16)
        return high, (w - high.astype(np.float64)).astype(np.float32).astype(jnp.bfloat16)

    def stacked(w):
        high, low = split(w)
        return np.concatenate([high, high, low])

    def squared(w):
        both = np.concatenate(split(w), axis=1)
        return np.concatenate([both, both])

    pool = np.concatenate([pool, pool], axis=1).reshape(-1, LANES).astype(jnp.bfloat16)
    turn_range, turn_pulse = np.asarray(turn_range, np.float32), np.asarray(turn_pulse, np.float32)
    pick = np.concatenate([pick, pick, pick], axis=1).astype(jnp.bfloat16)
    return [stacked(w1), stacked(w2), turn_range, squared(w3), squared(w4), turn_pulse, pool, pick]


def turned_quarter(re, im, sign):
    return (im, -re) if sign < 0 else (-im, re)


def dft4(x, sign):
    (r0, i0), (r1, i1), (r2, i2), (r3, i3) = x
    sr0, si0, dr0, di0 = r0 + r2, i0 + i2, r0 - r2, i0 - i2
    sr1, si1, dr1, di1 = r1 + r3, i1 + i3, r1 - r3, i1 - i3
    tr, ti = turned_quarter(dr1, di1, sign)
    return [(sr0 + sr1, si0 + si1), (dr0 + tr, di0 + ti), (sr0 - sr1, si0 - si1), (dr0 - tr, di0 - ti)]


def dft16(x, sign):
    stage = []
    for n2 in range(4):
        part = dft4([x[4 * n1 + n2] for n1 in range(4)], sign)
        moved = []
        for k1 in range(4):
            re, im = part[k1]
            if n2 * k1:
                angle = sign * 2.0 * math.pi * n2 * k1 / 16
                c, s = math.cos(angle), math.sin(angle)
                if n2 * k1 == 4:
                    re, im = turned_quarter(re, im, sign)
                else:
                    re, im = re * c - im * s, re * s + im * c
            moved.append((re, im))
        stage.append(moved)
    out = [None] * 16
    for k1 in range(4):
        last = dft4([stage[n2][k1] for n2 in range(4)], sign)
        for k2 in range(4):
            out[k1 + 4 * k2] = last[k2]
    return out


def swapped(v):
    return pltpu.roll(v, 64, 1)


def packed_dft4(x, unit):
    s0, d0, s1, d1 = x[0] + x[2], x[0] - x[2], x[1] + x[3], x[1] - x[3]
    t = swapped(d1) * unit
    return [s0 + s1, d0 + t, s0 - s1, d0 - t]


def packed_dft16(x, sign, unit):
    stage = []
    for n2 in range(4):
        part = packed_dft4([x[4 * n1 + n2] for n1 in range(4)], unit)
        moved = []
        for k1 in range(4):
            v = part[k1]
            if n2 * k1:
                angle = 2.0 * math.pi * n2 * k1 / 16
                c, s = math.cos(angle), math.sin(angle)
                v = swapped(v) * unit if n2 * k1 == 4 else v * c + swapped(v) * (unit * s)
            moved.append(v)
        stage.append(moved)
    out = [None] * 16
    for k1 in range(4):
        last = packed_dft4([stage[n2][k1] for n2 in range(4)], unit)
        for k2 in range(4):
            out[k1 + 4 * k2] = last[k2]
    return out


def halves(x):
    high = x.astype(jnp.bfloat16)
    return high, (x - high.astype(F32)).astype(jnp.bfloat16)


def dot(x, w, precision=None):
    return lax.dot_general(x, w, (((1,), (0,)), ((), ())), precision=precision, preferred_element_type=F32)


def dot_wide(x, w):
    high, low = halves(x)
    return dot(jnp.concatenate([high, low, high], axis=1), w)


def dot_square(x, w):
    y = dot(jnp.concatenate(halves(x), axis=1), w)
    return y[:, 0:128] + y[:, 128:256]


def dot_nt(x, w, precision=EXACT):
    return lax.dot_general(x, w, (((1,), (1,)), ((), ())), precision=precision, preferred_element_type=F32)


def kernel(
    raw, rfil, afil, inv, flags,
    w1_h, w2_h, tr_h, w3_h, w4_h, tp_h, pool_h, pick_h,
    out,
    x, rf, af, iv, mask, w1, w2, tr, w3, w4, tp, pool, pick,
    spec, gain, turned, sent, got, fcos, fsin, scene, stack, prod, look,
    wmine, wall, wide, edge_s, edge_r, border, low_s, low_r, slope, part_s, part_r,
    ld, ldx, s1, r1, s2, r2, s3, r3,
):
    a, s = lax.axis_index("acq"), lax.axis_index("strip")

    barrier = pltpu.get_barrier_semaphore()

    def greet(i, _):
        pl.semaphore_signal(barrier, inc=1, device_id=(a, lax.rem(s + i, DEV)), device_id_type=MESH)
        pl.semaphore_signal(barrier, inc=1, device_id=(lax.rem(a + i, DEV), s), device_id_type=MESH)
        return 0

    lax.fori_loop(1, DEV, greet, 0, unroll=True)

    def load_x(g):
        rows = pl.ds(pl.multiple_of(8 * g, 8), 8)
        return pltpu.make_async_copy(raw.at[0, :, rows, :], x.at[:, rows, :], ldx.at[g])

    loads = [
        pltpu.make_async_copy(src, dst, ld.at[i])
        for i, (src, dst) in enumerate([
            (rfil, rf), (tr_h, tr), (w1_h, w1), (w2_h, w2),
            (pick_h, pick), (afil, af), (inv, iv), (flags, mask), (w3_h, w3), (w4_h, w4), (tp_h, tp), (pool_h, pool),
        ])
    ]
    for copy in loads[:2]:
        copy.start()
    for g in range(8):
        load_x(g).start()
    for copy in loads[2:]:
        copy.start()

    lane = lax.broadcasted_iota(jnp.int32, (8, LANES), 1)
    row8 = lax.broadcasted_iota(jnp.int32, (8, LANES), 0)
    half = jnp.where(lane < 64, -1.0, 1.0).astype(F32)

    loads[0].wait()

    for c in range(2):
        for k in range(16):
            gain[pl.ds(16 * c + k, 1), pl.ds(0, 128)] = rf[pl.ds(c, 1), pl.ds(128 * k, 128)]
    eye = (lax.broadcasted_iota(jnp.int32, (128, 128), 0) == lax.broadcasted_iota(jnp.int32, (128, 128), 1)).astype(F32)
    across = dot_nt(eye, gain[:, pl.ds(0, 128)])
    to = lax.broadcasted_iota(jnp.int32, (32, 256), 1)
    meets = to // 8 == lax.broadcasted_iota(jnp.int32, (32, 256), 0)
    ordered = None
    for m in range(8):
        place = jnp.where(meets & (to % 8 == m), 1.0, 0.0).astype(F32)
        part = dot(across[16 * m : 16 * m + 16, :], place, EXACT)
        ordered = part if ordered is None else ordered + part
    gain[pl.ds(0, 16), :] = ordered
    loads[1].wait()

    def forward_range(g, _):
        load_x(g).wait()
        rows = pl.ds(pl.multiple_of(8 * g, 8), 8)
        field = [(x[0, rows, pl.ds(128 * n, 128)], x[1, rows, pl.ds(128 * n, 128)]) for n in range(16)]
        for k, (re, im) in enumerate(dft16(field, -1.0)):
            c, t = tr[pl.ds(k, 1), :], tr[pl.ds(16 + k, 1), :]
            at = pl.ds(pl.multiple_of(64 * k + 8 * g, 8), 8)
            spec[at, pl.ds(0, 128)] = re * c - im * t
            spec[at, pl.ds(128, 128)] = re * t + im * c
        return 0

    lax.fori_loop(0, 8, forward_range, 0, unroll=2)

    for copy in loads[2:4]:
        copy.wait()

    def filter_range(k, _):
        rows = pl.ds(pl.multiple_of(256 * k, 256), 256)
        z = dot_wide(spec[rows, :], w1[...])
        parts = []
        for i in range(4):
            g = gain[pl.ds(4 * k + i, 1), :]
            re, im = z[64 * i : 64 * i + 64, 0:128], z[64 * i : 64 * i + 64, 128:256]
            gr, gi = g[:, 0:128], g[:, 128:256]
            parts.append(jnp.concatenate([re * gr - im * gi, re * gi + im * gr], axis=1))
        y = dot_wide(jnp.concatenate(parts, axis=0), w2[...])
        for i in range(4):
            c, t = tr[pl.ds(32 + 4 * k + i, 1), :], tr[pl.ds(48 + 4 * k + i, 1), :]
            re, im = y[64 * i : 64 * i + 64, 0:128], y[64 * i : 64 * i + 64, 128:256]
            at = pl.ds(pl.multiple_of(256 * k + 64 * i, 64), 64)
            spec[at, pl.ds(0, 128)] = re * c - im * t
            spec[at, pl.ds(128, 128)] = re * t + im * c
        return 0

    lax.fori_loop(0, 4, filter_range, 0, unroll=True)

    def inverse_range(g, _):
        field = []
        for k in range(16):
            at = pl.ds(pl.multiple_of(64 * k + 8 * g, 8), 8)
            field.append((spec[at, pl.ds(0, 128)], spec[at, pl.ds(128, 128)]))
        for n, (re, im) in enumerate(dft16(field, 1.0)):
            turned[pl.ds(pl.multiple_of(128 * n + 8 * g, 8), 8), :] = re
            turned[pl.ds(pl.multiple_of(128 * n + 64 + 8 * g, 8), 8), :] = im
        return 0

    lax.fori_loop(0, 8, inverse_range, 0, unroll=2)

    def rows_of(block, tile, count):
        return pl.ds(pl.multiple_of(128 * block + 8 * tile, 8), 8 * count)

    def strip_copy(u, tile, count, i):
        p = lax.rem(s + i, DEV)
        return pltpu.make_async_remote_copy(
            src_ref=sent.at[rows_of(p, tile, count), :], dst_ref=got.at[rows_of(s, tile, count), :],
            send_sem=s1.at[0], recv_sem=r1.at[u], device_id=(a, p), device_id_type=MESH,
        )

    def acq_copy(u, tile, count, i):
        p = lax.rem(a + i, DEV)
        return pltpu.make_async_remote_copy(
            src_ref=scene.at[rows_of(p, tile, count), :], dst_ref=stack.at[rows_of(a, tile, count), :],
            send_sem=s2.at[0], recv_sem=r2.at[u], device_id=(p, s), device_id_type=MESH,
        )

    def weight_copy(i):
        p = lax.rem(a + i, DEV)
        return pltpu.make_async_remote_copy(
            src_ref=wmine, dst_ref=wall.at[pl.ds(pl.multiple_of(8 * a, 8), 8), :],
            send_sem=s3.at[0], recv_sem=r3.at[0], device_id=(p, s), device_id_type=MESH,
        )

    def part_copy(i):
        p = lax.rem(a + i, DEV)
        return pltpu.make_async_remote_copy(
            src_ref=part_s.at[pl.ds(pl.multiple_of(8 * p, 8), 8), :],
            dst_ref=part_r.at[pl.ds(pl.multiple_of(8 * a, 8), 8), :],
            send_sem=s3.at[1], recv_sem=r3.at[1], device_id=(p, s), device_id_type=MESH,
        )

    def edge_copy(i):
        p = lax.rem(a + i, DEV)
        return pltpu.make_async_remote_copy(
            src_ref=edge_s.at[pl.ds(pl.multiple_of(8 * p, 8), 8), :],
            dst_ref=edge_r.at[pl.ds(pl.multiple_of(8 * a, 8), 8), :],
            send_sem=s3.at[3], recv_sem=r3.at[3], device_id=(p, s), device_id_type=MESH,
        )

    def wait_rows(ref, count, sem):
        rows = ref.at[pl.ds(0, 15 * count), :]
        pltpu.make_async_copy(rows, rows, sem).wait()

    def others(body):
        for i in ORDER:
            body(i)

    for n in range(16):
        sent[pl.ds(128 * n, 128), :] = turned[pl.ds(128 * n, 128), :].T
    pl.semaphore_wait(barrier, 2 * (DEV - 1))
    for u, (tile, count) in enumerate(UNITS):
        others(lambda i, u=u, tile=tile, count=count: strip_copy(u, tile, count, i).start())
    own = pl.ds(pl.multiple_of(128 * s, 128), 128)
    got[own, :] = sent[own, :]

    for copy in loads[4:]:
        copy.wait()

    def turn_filter(k, _):
        re, im = af[0, pl.ds(k, 64, stride=16), :], af[1, pl.ds(k, 64, stride=16), :]
        both = jnp.concatenate([re, im], axis=0)
        b0 = both.astype(jnp.bfloat16)
        left = both - b0.astype(F32)
        b1 = left.astype(jnp.bfloat16)
        b2 = (left - b1.astype(F32)).astype(jnp.bfloat16)
        v = dot_nt(pick[...], jnp.concatenate([b0, b1, b2], axis=1), None)
        w = swapped(v)
        first = lax.broadcasted_iota(jnp.int32, (128, 128), 1) < 64
        c = jnp.where(first, v, w)
        t = jnp.where(first, -w, v)
        for q in range(TILES):
            at = pl.ds(pl.multiple_of(128 * q + 8 * k, 8), 8)
            fcos[at, :] = c[8 * q : 8 * q + 8, :]
            fsin[at, :] = t[8 * q : 8 * q + 8, :]
        return 0

    lax.fori_loop(0, 16, turn_filter, 0)

    usable = [jnp.where(a >= l + 1, mask[0, l].astype(F32), 0.0) for l in range(2)]
    wmine[...] = jnp.zeros((8, LANES), F32)
    for l in range(2):
        wmine[pl.ds(l, 1), pl.ds(0, DEV)] = iv[pl.ds(l, 1), :] * usable[l]

    others(lambda i: weight_copy(i).start())
    wall[pl.ds(pl.multiple_of(8 * a, 8), 8), :] = wmine[...]

    def azimuth(tile, count):
        parts = []
        for m in range(count):
            field = [got[rows_of(n, tile + m, 1), :] for n in range(16)]
            for k, v in enumerate(packed_dft16(field, -1.0, -half)):
                parts.append(v * tp[pl.ds(k, 1), :] + swapped(v) * tp[pl.ds(16 + k, 1), :])
        at = pl.ds(pl.multiple_of(128 * tile, 128), 128 * count)
        z = dot_square(jnp.concatenate(parts, axis=0), w3[...])
        z = z * fcos[at, :] + swapped(z) * fsin[at, :]
        z = dot_square(z, w4[...])
        z2 = swapped(z)
        for m in range(count):
            field = []
            for k in range(16):
                piece = slice(128 * m + 8 * k, 128 * m + 8 * k + 8)
                field.append(z[piece, :] * tp[pl.ds(32 + k, 1), :] + z2[piece, :] * tp[pl.ds(48 + k, 1), :])
            for n, v in enumerate(packed_dft16(field, 1.0, half)):
                scene[rows_of(n, tile + m, 1), :] = v

    def edges(tile, count):
        for m in range(count):
            t = tile + m
            for n in range(1, 16):
                v = scene[rows_of(n, t, 1), :]
                v = jnp.where(lane % 8 < 4, pltpu.roll(v, 8 * t, 1), pltpu.roll(v, lax.rem(8 * t + 68, 128), 1))
                at = pl.ds(8 * (n - 1), 8)
                edge_s[at, :] = jnp.where(lane // 8 == t, v, edge_s[at, :])

    def products(tile, count):
        held = {}
        for j in range(DEV):
            held[j] = [stack[rows_of(j, tile + m, 1), :] for m in range(count)]
            later = [swapped(v) for v in held[j]]
            for l in (1, 2):
                if j >= l:
                    same, cross = None, None
                    for m in range(count):
                        v, w = held[j - l][m] * held[j][m], held[j - l][m] * later[m]
                        same, cross = (v, w) if same is None else (same + v, cross + w)
                    p = PAIRS.index((l, j))
                    prod[pl.ds(8 * p, 8), pl.ds(0, 128)] = same
                    prod[pl.ds(8 * p, 8), pl.ds(128, 128)] = cross
        block = pl.ds(pl.multiple_of(512 * (tile // 4), 512), 512)
        pooled = dot(jnp.concatenate(halves(prod[...]), axis=1), pool[block, :])
        look[...] += pooled

    def focus(u, tile, count):
        wait_rows(got, 8 * count, r1.at[u])
        azimuth(tile, count)
        others(lambda i: acq_copy(u, tile, count, i).start())
        edges(tile, count)
        stack[rows_of(a, tile, count), :] = scene[rows_of(a, tile, count), :]

    def combine(u, tile, count):
        wait_rows(stack, 8 * count, r2.at[u])
        products(tile, count)

    look[...] = jnp.zeros_like(look)
    edge_s[...] = jnp.zeros_like(edge_s)

    def turn(u, _):
        focus(u, 4 * u, 4)

        @pl.when(u == 1)
        def _():
            combine(0, 0, 4)

        return 0

    lax.fori_loop(0, LONG, turn, 0)

    low_s[...] = jnp.zeros_like(low_s)
    low_s[pl.ds(0, len(PAIRS)), :] = look[pl.ds(0, len(PAIRS), stride=8), :]
    low_copy = pltpu.make_async_remote_copy(
        src_ref=low_s, dst_ref=low_r, send_sem=s3.at[2], recv_sem=r3.at[2],
        device_id=(a, lax.rem(s + DEV - 1, DEV)), device_id_type=MESH,
    )

    @pl.when(s > 0)
    def _():
        low_copy.start()

    for u in range(LONG, len(UNITS)):
        focus(u, *UNITS[u])
    others(lambda i: edge_copy(i).start())
    mine = pl.ds(pl.multiple_of(8 * a, 8), 8)
    edge_r[mine, :] = edge_s[mine, :]
    wait_rows(wall, 8, r3.at[0])
    for l in range(2):
        columns = wall[pl.ds(l, 16, stride=8), :]
        for e in range(DEV):
            wide[pl.ds(16 * (16 * l + e), 16), :] = jnp.broadcast_to(columns[:, e : e + 1], (16, LANES))

    for u in range(1, len(UNITS)):
        combine(u, *UNITS[u])

    wait_rows(edge_r, 8, r3.at[3])
    edge = [edge_r[pl.ds(8 * j, 8), :] for j in range(DEV)]
    turned_edge = [jnp.where(lane % 8 < 4, pltpu.roll(v, 124, 1), pltpu.roll(v, 4, 1)) for v in edge]
    for p, (l, j) in enumerate(PAIRS):
        prod[pl.ds(8 * p, 8), pl.ds(0, 128)] = edge[j - l] * edge[j]
        prod[pl.ds(8 * p, 8), pl.ds(128, 128)] = edge[j - l] * turned_edge[j]
    border[...] = dot(jnp.concatenate(halves(prod[...]), axis=1), pool[pl.ds(512 * CHUNKS, 512), :])

    above = s < DEV - 1

    @pl.when(above)
    def _():
        low_copy.wait_recv()

    low_r[...] = jnp.where(above, pltpu.roll(low_r[...], 112, 1), 0.0)
    last_look = lane % 16 == 15
    corner = (row8 == 7) & (lane % 64 >= 48)
    for p in range(len(PAIRS)):
        v = look[pl.ds(8 * p, 8), :]
        after = pltpu.roll(v, 63, 1)
        after = jnp.where(last_look, border[pl.ds(8 * p, 8), :], after)
        up = jnp.where(row8 == 0, pltpu.roll(v, 48, 1), pltpu.roll(v, 64, 1))
        up = pltpu.roll(up, 7, 0)
        up = jnp.where(corner, jnp.broadcast_to(low_r[pl.ds(p, 1), :], (8, LANES)), up)
        w = v * -half
        azim, rang = w * after, w * up
        slope[pl.ds(8 * p, 8), :] = jnp.where(lane < 64, azim, rang) + pltpu.roll(
            jnp.where(lane < 64, rang, azim), 64, 1
        )

    total = [None] * DEV
    for p, (l, j) in enumerate(PAIRS):
        v = slope[pl.ds(8 * p, 8), :]
        for e in range(DEV):
            term = wide[pl.ds(16 * (16 * (l - 1) + e) + j, 1), :] * v
            total[e] = term if total[e] is None else total[e] + term
    for e in range(DEV):
        part_s[pl.ds(8 * e, 8), :] = total[e]
    others(lambda i: part_copy(i).start())
    part_r[mine, :] = part_s[mine, :]
    wait_rows(part_r, 8, r3.at[1])

    for d in range(2):
        for h in range(CHUNKS):
            for u in range(2):
                tile = None
                for t in range(8):
                    v = part_r[pl.ds(8 * (8 * u + t), 8), :]
                    shift = 16 * (t - 4 * d - h) % 128
                    v = pltpu.roll(v, shift, 1) if shift else v
                    tile = v if tile is None else jnp.where(lane // 16 == t, v, tile)
                out[0, d, pl.ds(8 * h, 8), pl.ds(128 * u, 128)] = tile

    wait_rows(sent, 128, s1.at[0])
    wait_rows(scene, 128, s2.at[0])
    wait_rows(wall, 8, s3.at[0])
    wait_rows(part_s, 8, s3.at[1])
    wait_rows(edge_s, 8, s3.at[3])

    @pl.when(s > 0)
    def _():
        low_copy.wait_send()


def per_device(raw_echoes, range_filter, azimuth_filter, pair_mask, inversion):
    consts = tables()
    hbm = pl.BlockSpec(memory_space=pl.ANY)
    vmem = lambda *shape: pltpu.VMEM(shape, F32)
    dma = pltpu.SemaphoreType.DMA
    return pl.pallas_call(
        kernel,
        out_shape=pltpu.VMEM((1, 2, WIDE, 256), F32),
        in_specs=[hbm] * 5 + [hbm] * len(consts),
        out_specs=pl.BlockSpec(memory_space=pltpu.VMEM),
        scratch_shapes=[vmem(2, 64, 2048), vmem(2, 2048), vmem(2, 1024, 128), vmem(2, DEV), pltpu.SMEM((1, 2), jnp.int32)]
        + [pltpu.VMEM(c.shape, c.dtype) for c in consts]
        + [
            vmem(1024, 256), vmem(32, 256), vmem(2048, 128), vmem(2048, 128), vmem(2048, 128),
            vmem(2048, 128), vmem(2048, 128), vmem(2048, 128), vmem(2048, 128),
            vmem(ROWS, 256), vmem(ROWS, 128),
            vmem(8, 128), vmem(128, 128), vmem(512, 128), vmem(128, 128), vmem(128, 128), vmem(ROWS, 128), vmem(32, 128), vmem(32, 128),
            vmem(ROWS, 128), vmem(128, 128), vmem(128, 128),
            dma((12,)), dma((8,)), dma((1,)), dma((len(UNITS),)), dma((1,)), dma((len(UNITS),)), dma((4,)), dma((4,)),
        ],
        compiler_params=pltpu.CompilerParams(collective_id=0, has_side_effects=True, vmem_limit_bytes=60 * 1024 * 1024),
    )(raw_echoes, range_filter, azimuth_filter, inversion[:, 0, :].T, pair_mask, *[jnp.asarray(c) for c in consts])


def solution(mesh):
    return jax.shard_map(
        per_device,
        mesh=mesh,
        in_specs=(
            P("acq", None, "strip", None),
            P(),
            P(None, None, "strip"),
            P("acq", None),
            P(None, "acq", None),
        ),
        out_specs=P("acq", None, "strip", None),
        check_vma=False,
    )
```

```python
import functools
import math

import jax
import jax.numpy as jnp
import numpy as np
from jax import lax
from jax.experimental import pallas as pl
from jax.experimental.pallas import tpu as pltpu
from jax.sharding import PartitionSpec as P

MESH = pl.DeviceIdType.MESH
EXACT = lax.Precision.HIGHEST
F32 = jnp.float32
LANES = 128
DEV = 16
ORDER = (8, 7, 9, 6, 10, 5, 11, 4, 12, 3, 13, 2, 14, 1, 15)
ZS = 8
Q = 64
CHUNKS = 4
WIDE = 32
TILES = 16
LONG = 3
UNITS = [(4 * u, 4) for u in range(LONG)] + [(12, 3), (15, 1)]
PAIRS = [(1, j) for j in range(1, DEV)] + [(2, j) for j in range(2, DEV)]
ROWS = 8 * len(PAIRS)


def block_table(size, sign, scale=1.0):
    index = np.arange(size)
    angle = sign * 2.0 * math.pi / size * (index[:, None] * index[None, :] % size)
    cosine, sine = np.cos(angle) * scale, np.sin(angle) * scale
    return np.block([[cosine, sine], [-sine, cosine]])


def turn_table(count, width, size, sign):
    angle = sign * 2.0 * math.pi / size * (np.arange(count)[:, None] * np.arange(width)[None, :] % size)
    return np.cos(angle), np.sin(angle)


def sample_order():
    order = np.zeros(LANES, dtype=np.int64)
    for h in range(CHUNKS):
        for m in range(4):
            for k in range(8):
                order[WIDE * h + 8 * m + k] = WIDE * h + 4 * k + m
    return order


def tables():
    order = sample_order()
    w1 = block_table(128, -1.0)
    w2 = block_table(128, 1.0, 1.0 / 2048)
    w2 = w2[:, np.concatenate([order, 128 + order])]
    c1, s1 = turn_table(16, 128, 2048, -1.0)
    c2, s2 = turn_table(16, 128, 2048, 1.0)
    turn_range = np.concatenate([c1, s1, c2[:, order], s2[:, order]])
    w3 = block_table(64, -1.0)
    w4 = block_table(64, 1.0, 1.0 / 1024)
    c3, s3 = turn_table(16, 64, 1024, -1.0)
    c4, s4 = turn_table(16, 64, 1024, 1.0)
    turn_pulse = np.concatenate(
        [np.hstack([c3, c3]), np.hstack([-s3, s3]), np.hstack([c4, c4]), np.hstack([-s4, s4])]
    )
    pool = np.zeros((CHUNKS + 1, 256, LANES))
    for h in range(CHUNKS):
        for q in range(Q):
            real, imag = 16 * h + q // 4, 64 + 16 * h + q // 4
            pool[h, q, real] = 0.25
            pool[h, 64 + q, real] = 0.25
            pool[h, 128 + q, imag] = -0.25
            pool[h, 192 + q, imag] = 0.25
    for lane in range(LANES):
        at = 16 * (lane // 32) + 15
        pool[CHUNKS, lane, 64 + at] = 0.25
        pool[CHUNKS, 128 + lane, at] = -0.25 if lane % 8 < 4 else 0.25
    pick = np.zeros((LANES, LANES))
    pick[np.arange(LANES), order] = 1.0
    def split(w):
        high = np.asarray(w, np.float32).astype(jnp.bfloat16)
        return high, (w - high.astype(np.float64)).astype(np.float32).astype(jnp.bfloat16)

    def stacked(w):
        high, low = split(w)
        return np.concatenate([high, high, low])

    def squared(w):
        both = np.concatenate(split(w), axis=1)
        return np.concatenate([both, both])

    pool = np.concatenate([pool, pool], axis=1).reshape(-1, LANES).astype(jnp.bfloat16)
    turn_range, turn_pulse = np.asarray(turn_range, np.float32), np.asarray(turn_pulse, np.float32)
    pick = np.concatenate([pick, pick, pick], axis=1).astype(jnp.bfloat16)
    return [stacked(w1), stacked(w2), turn_range, squared(w3), squared(w4), turn_pulse, pool, pick]


def turned_quarter(re, im, sign):
    return (im, -re) if sign < 0 else (-im, re)


def dft4(x, sign):
    (r0, i0), (r1, i1), (r2, i2), (r3, i3) = x
    sr0, si0, dr0, di0 = r0 + r2, i0 + i2, r0 - r2, i0 - i2
    sr1, si1, dr1, di1 = r1 + r3, i1 + i3, r1 - r3, i1 - i3
    tr, ti = turned_quarter(dr1, di1, sign)
    return [(sr0 + sr1, si0 + si1), (dr0 + tr, di0 + ti), (sr0 - sr1, si0 - si1), (dr0 - tr, di0 - ti)]


def dft16(x, sign):
    stage = []
    for n2 in range(4):
        part = dft4([x[4 * n1 + n2] for n1 in range(4)], sign)
        moved = []
        for k1 in range(4):
            re, im = part[k1]
            if n2 * k1:
                angle = sign * 2.0 * math.pi * n2 * k1 / 16
                c, s = math.cos(angle), math.sin(angle)
                if n2 * k1 == 4:
                    re, im = turned_quarter(re, im, sign)
                else:
                    re, im = re * c - im * s, re * s + im * c
            moved.append((re, im))
        stage.append(moved)
    out = [None] * 16
    for k1 in range(4):
        last = dft4([stage[n2][k1] for n2 in range(4)], sign)
        for k2 in range(4):
            out[k1 + 4 * k2] = last[k2]
    return out


def swapped(v):
    return pltpu.roll(v, 64, 1)


def packed_dft4(x, unit):
    s0, d0, s1, d1 = x[0] + x[2], x[0] - x[2], x[1] + x[3], x[1] - x[3]
    t = swapped(d1) * unit
    return [s0 + s1, d0 + t, s0 - s1, d0 - t]


def packed_dft16(x, sign, unit):
    stage = []
    for n2 in range(4):
        part = packed_dft4([x[4 * n1 + n2] for n1 in range(4)], unit)
        moved = []
        for k1 in range(4):
            v = part[k1]
            if n2 * k1:
                angle = 2.0 * math.pi * n2 * k1 / 16
                c, s = math.cos(angle), math.sin(angle)
                v = swapped(v) * unit if n2 * k1 == 4 else v * c + swapped(v) * (unit * s)
            moved.append(v)
        stage.append(moved)
    out = [None] * 16
    for k1 in range(4):
        last = packed_dft4([stage[n2][k1] for n2 in range(4)], unit)
        for k2 in range(4):
            out[k1 + 4 * k2] = last[k2]
    return out


def halves(x):
    high = x.astype(jnp.bfloat16)
    return high, (x - high.astype(F32)).astype(jnp.bfloat16)


def dot(x, w, precision=None):
    return lax.dot_general(x, w, (((1,), (0,)), ((), ())), precision=precision, preferred_element_type=F32)


def dot_wide(x, w):
    high, low = halves(x)
    return dot(jnp.concatenate([high, low, high], axis=1), w)


def dot_square(x, w):
    y = dot(jnp.concatenate(halves(x), axis=1), w)
    return y[:, 0:128] + y[:, 128:256]


def dot_nt(x, w, precision=EXACT):
    return lax.dot_general(x, w, (((1,), (1,)), ((), ())), precision=precision, preferred_element_type=F32)


def kernel(
    raw, rfil, afil, inv, flags,
    w1_h, w2_h, tr_h, w3_h, w4_h, tp_h, pool_h, pick_h,
    out,
    x, rf, af, iv, mask, w1, w2, tr, w3, w4, tp, pool, pick,
    spec, gain, turned, sent, flip_s, flip_r, got, fcos, fsin, scene, stack, prod, cross, look,
    wmine, wall, wide, edge_s, edge_r, border, low_s, low_r, slope, part_s, part_r,
    ld, ldx, s1, r1, s2, r2, s3, r3, s4, r4,
):
    a, s = lax.axis_index("acq"), lax.axis_index("strip")

    z, xh = lax.rem(s, ZS), s // ZS
    partner = (1 - xh) * ZS + z

    barrier = pltpu.get_barrier_semaphore()

    def greet(device):
        pl.semaphore_signal(barrier, inc=1, device_id=device, device_id_type=MESH)

    for i in (4, 3, 5, 2, 6, 1, 7):
        greet((a, xh * ZS + lax.rem(z + i, ZS)))
    for i in ORDER:
        greet((lax.rem(a + i, DEV), s))
    greet((a, partner))

    @pl.when(z == ZS - 1)
    def _():
        greet((a, (1 - xh) * ZS))

    @pl.when(z == 0)
    def _():
        greet((a, (1 - xh) * ZS + ZS - 1))

    def load_x(g):
        rows = pl.ds(pl.multiple_of(8 * g, 8), 8)
        return pltpu.make_async_copy(raw.at[0, :, rows, :], x.at[:, rows, :], ldx.at[g])

    loads = [
        pltpu.make_async_copy(src, dst, ld.at[i])
        for i, (src, dst) in enumerate([
            (rfil, rf), (tr_h, tr), (w1_h, w1), (w2_h, w2),
            (pick_h, pick), (afil, af), (inv, iv), (flags, mask), (w3_h, w3), (w4_h, w4), (tp_h, tp), (pool_h, pool),
        ])
    ]
    for copy in loads[:2]:
        copy.start()
    for g in range(8):
        load_x(g).start()
    for copy in loads[2:]:
        copy.start()

    lane = lax.broadcasted_iota(jnp.int32, (8, LANES), 1)
    row8 = lax.broadcasted_iota(jnp.int32, (8, LANES), 0)
    half = jnp.where(lane < 64, -1.0, 1.0).astype(F32)

    loads[0].wait()

    for c in range(2):
        for k in range(16):
            gain[pl.ds(16 * c + k, 1), pl.ds(0, 128)] = rf[pl.ds(c, 1), pl.ds(128 * k, 128)]
    eye = (lax.broadcasted_iota(jnp.int32, (128, 128), 0) == lax.broadcasted_iota(jnp.int32, (128, 128), 1)).astype(F32)
    across = dot_nt(eye, gain[:, pl.ds(0, 128)])
    to = lax.broadcasted_iota(jnp.int32, (32, 256), 1)
    meets = to // 8 == lax.broadcasted_iota(jnp.int32, (32, 256), 0)
    ordered = None
    for m in range(8):
        place = jnp.where(meets & (to % 8 == m), 1.0, 0.0).astype(F32)
        part = dot(across[16 * m : 16 * m + 16, :], place, EXACT)
        ordered = part if ordered is None else ordered + part
    gain[pl.ds(0, 16), :] = ordered
    loads[1].wait()

    def forward_range(g, _):
        load_x(g).wait()
        rows = pl.ds(pl.multiple_of(8 * g, 8), 8)
        field = [(x[0, rows, pl.ds(128 * n, 128)], x[1, rows, pl.ds(128 * n, 128)]) for n in range(16)]
        for k, (re, im) in enumerate(dft16(field, -1.0)):
            c, t = tr[pl.ds(k, 1), :], tr[pl.ds(16 + k, 1), :]
            at = pl.ds(pl.multiple_of(64 * k + 8 * g, 8), 8)
            spec[at, pl.ds(0, 128)] = re * c - im * t
            spec[at, pl.ds(128, 128)] = re * t + im * c
        return 0

    lax.fori_loop(0, 8, forward_range, 0, unroll=2)

    for copy in loads[2:4]:
        copy.wait()

    def filter_range(k, _):
        rows = pl.ds(pl.multiple_of(256 * k, 256), 256)
        z = dot_wide(spec[rows, :], w1[...])
        parts = []
        for i in range(4):
            g = gain[pl.ds(4 * k + i, 1), :]
            re, im = z[64 * i : 64 * i + 64, 0:128], z[64 * i : 64 * i + 64, 128:256]
            gr, gi = g[:, 0:128], g[:, 128:256]
            parts.append(jnp.concatenate([re * gr - im * gi, re * gi + im * gr], axis=1))
        y = dot_wide(jnp.concatenate(parts, axis=0), w2[...])
        for i in range(4):
            c, t = tr[pl.ds(32 + 4 * k + i, 1), :], tr[pl.ds(48 + 4 * k + i, 1), :]
            re, im = y[64 * i : 64 * i + 64, 0:128], y[64 * i : 64 * i + 64, 128:256]
            at = pl.ds(pl.multiple_of(256 * k + 64 * i, 64), 64)
            spec[at, pl.ds(0, 128)] = re * c - im * t
            spec[at, pl.ds(128, 128)] = re * t + im * c
        return 0

    lax.fori_loop(0, 4, filter_range, 0, unroll=True)

    def inverse_range(g, _):
        field = []
        for k in range(16):
            at = pl.ds(pl.multiple_of(64 * k + 8 * g, 8), 8)
            field.append((spec[at, pl.ds(0, 128)], spec[at, pl.ds(128, 128)]))
        for n, (re, im) in enumerate(dft16(field, 1.0)):
            turned[pl.ds(pl.multiple_of(128 * n + 8 * g, 8), 8), :] = re
            turned[pl.ds(pl.multiple_of(128 * n + 64 + 8 * g, 8), 8), :] = im
        return 0

    lax.fori_loop(0, 8, inverse_range, 0, unroll=2)

    def rows_of(block, tile, count):
        return pl.ds(pl.multiple_of(128 * block + 8 * tile, 8), 8 * count)

    def direct_copy(u, tile, count, i):
        p = lax.rem(z + i, ZS)
        return pltpu.make_async_remote_copy(
            src_ref=sent.at[rows_of(p, tile, count), :], dst_ref=got.at[rows_of(s, tile, count), :],
            send_sem=s1.at[0], recv_sem=r1.at[u], device_id=(a, xh * ZS + p), device_id_type=MESH,
        )

    def flip_copy(u, tile, count):
        rows = pl.ds(64 * tile, 64 * count)
        return pltpu.make_async_remote_copy(
            src_ref=flip_s.at[rows, :], dst_ref=flip_r.at[rows, :],
            send_sem=s4.at[0], recv_sem=r4.at[u], device_id=(a, partner), device_id_type=MESH,
        )

    def flip_rows(tile, count, p):
        return pl.ds(pl.multiple_of(64 * tile + 8 * count * p, 8), 8 * count)

    def relay_copy(u, tile, count, i):
        p = lax.rem(z + i, ZS)
        return pltpu.make_async_remote_copy(
            src_ref=flip_r.at[flip_rows(tile, count, p), :], dst_ref=got.at[rows_of(partner, tile, count), :],
            send_sem=s1.at[0], recv_sem=r1.at[u], device_id=(a, xh * ZS + p), device_id_type=MESH,
        )

    def acq_copy(u, tile, count, i):
        p = lax.rem(a + i, DEV)
        return pltpu.make_async_remote_copy(
            src_ref=scene.at[rows_of(p, tile, count), :], dst_ref=stack.at[rows_of(a, tile, count), :],
            send_sem=s2.at[0], recv_sem=r2.at[u], device_id=(p, s), device_id_type=MESH,
        )

    def weight_copy(i):
        p = lax.rem(a + i, DEV)
        return pltpu.make_async_remote_copy(
            src_ref=wmine, dst_ref=wall.at[pl.ds(pl.multiple_of(8 * a, 8), 8), :],
            send_sem=s3.at[0], recv_sem=r3.at[0], device_id=(p, s), device_id_type=MESH,
        )

    def part_copy(i):
        p = lax.rem(a + i, DEV)
        return pltpu.make_async_remote_copy(
            src_ref=part_s.at[pl.ds(pl.multiple_of(8 * p, 8), 8), :],
            dst_ref=part_r.at[pl.ds(pl.multiple_of(8 * a, 8), 8), :],
            send_sem=s3.at[1], recv_sem=r3.at[1], device_id=(p, s), device_id_type=MESH,
        )

    def edge_copy(i):
        p = lax.rem(a + i, DEV)
        return pltpu.make_async_remote_copy(
            src_ref=edge_s.at[pl.ds(pl.multiple_of(8 * p, 8), 8), :],
            dst_ref=edge_r.at[pl.ds(pl.multiple_of(8 * a, 8), 8), :],
            send_sem=s3.at[3], recv_sem=r3.at[3], device_id=(p, s), device_id_type=MESH,
        )

    def wait_rows(ref, count, sem, times=DEV - 1):
        rows = ref.at[pl.ds(0, times * count), :]
        pltpu.make_async_copy(rows, rows, sem).wait()

    def others(body):
        for i in ORDER:
            body(i)

    for n in range(ZS):
        v = turned[pl.ds(pl.multiple_of(128 * (ZS * (1 - xh) + n), 128), 128), :].T
        for tile, count in UNITS:
            flip_s[pl.ds(64 * tile + 8 * count * n, 8 * count), :] = v[8 * tile : 8 * tile + 8 * count, :]
    for n in range(ZS):
        sent[pl.ds(128 * n, 128), :] = turned[pl.ds(pl.multiple_of(128 * (ZS * xh + n), 128), 128), :].T
    pl.semaphore_wait(barrier, ZS + DEV - 1 + jnp.where((z == 0) | (z == ZS - 1), 1, 0))

    def direct(u):
        for i in (4, 3, 5, 2, 6, 1, 7):
            direct_copy(u, *UNITS[u], i).start()

    def relay(u):
        tile, count = UNITS[u]
        flip_copy(u, tile, count).wait_recv()
        for i in (4, 3, 5, 2, 6, 1, 7):
            relay_copy(u, tile, count, i).start()
        got[rows_of(partner, tile, count), :] = flip_r[flip_rows(tile, count, z), :]

    flip_copy(0, *UNITS[0]).start()
    direct(0)
    for u in range(1, len(UNITS)):
        flip_copy(u, *UNITS[u]).start()
    direct(1)
    got[pl.ds(pl.multiple_of(128 * s, 128), 128), :] = sent[pl.ds(pl.multiple_of(128 * z, 128), 128), :]

    for copy in loads[4:]:
        copy.wait()

    def turn_filter(k, _):
        re, im = af[0, pl.ds(k, 64, stride=16), :], af[1, pl.ds(k, 64, stride=16), :]
        both = jnp.concatenate([re, im], axis=0)
        b0 = both.astype(jnp.bfloat16)
        left = both - b0.astype(F32)
        b1 = left.astype(jnp.bfloat16)
        b2 = (left - b1.astype(F32)).astype(jnp.bfloat16)
        v = dot_nt(pick[...], jnp.concatenate([b0, b1, b2], axis=1), None)
        w = swapped(v)
        first = lax.broadcasted_iota(jnp.int32, (128, 128), 1) < 64
        c = jnp.where(first, v, w)
        t = jnp.where(first, -w, v)
        for q in range(TILES):
            at = pl.ds(pl.multiple_of(128 * q + 8 * k, 8), 8)
            fcos[at, :] = c[8 * q : 8 * q + 8, :]
            fsin[at, :] = t[8 * q : 8 * q + 8, :]
        return 0

    lax.fori_loop(0, 16, turn_filter, 0)

    relay(0)
    direct(2)
    relay(1)
    relay(2)
    for u in range(LONG, len(UNITS)):
        direct(u)

    usable = [jnp.where(a >= l + 1, mask[0, l].astype(F32), 0.0) for l in range(2)]
    wmine[...] = jnp.zeros((8, LANES), F32)
    for l in range(2):
        wmine[pl.ds(l, 1), pl.ds(0, DEV)] = iv[pl.ds(l, 1), :] * usable[l]

    others(lambda i: weight_copy(i).start())
    wall[pl.ds(pl.multiple_of(8 * a, 8), 8), :] = wmine[...]

    def azimuth(tile, count):
        parts = []
        for m in range(count):
            field = [got[rows_of(n, tile + m, 1), :] for n in range(16)]
            for k, v in enumerate(packed_dft16(field, -1.0, -half)):
                parts.append(v * tp[pl.ds(k, 1), :] + swapped(v) * tp[pl.ds(16 + k, 1), :])
        at = pl.ds(pl.multiple_of(128 * tile, 128), 128 * count)
        z = dot_square(jnp.concatenate(parts, axis=0), w3[...])
        z = z * fcos[at, :] + swapped(z) * fsin[at, :]
        z = dot_square(z, w4[...])
        z2 = swapped(z)
        for m in range(count):
            field = []
            for k in range(16):
                piece = slice(128 * m + 8 * k, 128 * m + 8 * k + 8)
                field.append(z[piece, :] * tp[pl.ds(32 + k, 1), :] + z2[piece, :] * tp[pl.ds(48 + k, 1), :])
            for n, v in enumerate(packed_dft16(field, 1.0, half)):
                scene[rows_of(n, tile + m, 1), :] = v

    def edges(tile, count):
        for m in range(count):
            t = tile + m
            for n in range(1, 16):
                v = scene[rows_of(n, t, 1), :]
                v = jnp.where(lane % 8 < 4, pltpu.roll(v, 8 * t, 1), pltpu.roll(v, lax.rem(8 * t + 68, 128), 1))
                at = pl.ds(8 * (n - 1), 8)
                edge_s[at, :] = jnp.where(lane // 8 == t, v, edge_s[at, :])

    def products(tile, count):
        held = {}
        for j in range(DEV):
            held[j] = [stack[rows_of(j, tile + m, 1), :] for m in range(count)]
            later = [swapped(v) for v in held[j]]
            for l in (1, 2):
                if j >= l:
                    same, other = None, None
                    for m in range(count):
                        v, w = held[j - l][m] * held[j][m], held[j - l][m] * later[m]
                        same, other = (v, w) if same is None else (same + v, other + w)
                    p = PAIRS.index((l, j))
                    prod[pl.ds(8 * p, 8), pl.ds(0, 128)] = same
                    prod[pl.ds(8 * p, 8), pl.ds(128, 128)] = other
        block = pl.ds(pl.multiple_of(512 * (tile // 4), 512), 512)
        pooled = dot(jnp.concatenate(halves(prod[...]), axis=1), pool[block, :])
        look[...] += pooled

    def focus(u, tile, count):
        wait_rows(got, 8 * count, r1.at[u], 2 * ZS - 2)
        azimuth(tile, count)
        others(lambda i: acq_copy(u, tile, count, i).start())
        edges(tile, count)
        stack[rows_of(a, tile, count), :] = scene[rows_of(a, tile, count), :]

    def combine(u, tile, count):
        wait_rows(stack, 8 * count, r2.at[u])
        products(tile, count)

    look[...] = jnp.zeros_like(look)
    edge_s[...] = jnp.zeros_like(edge_s)

    def turn(u, _):
        focus(u, 4 * u, 4)

        @pl.when(u == 0)
        def _():
            for later in range(LONG, len(UNITS)):
                relay(later)

        @pl.when(u == 1)
        def _():
            combine(0, 0, 4)

        return 0

    lax.fori_loop(0, LONG, turn, 0)

    low_s[...] = jnp.zeros_like(low_s)
    low_s[pl.ds(0, len(PAIRS)), :] = look[pl.ds(0, len(PAIRS), stride=8), :]
    low_copy = pltpu.make_async_remote_copy(
        src_ref=low_s, dst_ref=low_r, send_sem=s3.at[2], recv_sem=r3.at[2],
        device_id=(a, lax.rem(s + DEV - 1, DEV)), device_id_type=MESH,
    )

    @pl.when(s > 0)
    def _():
        low_copy.start()

    for u in range(LONG, len(UNITS)):
        focus(u, *UNITS[u])
    others(lambda i: edge_copy(i).start())
    mine = pl.ds(pl.multiple_of(8 * a, 8), 8)
    edge_r[mine, :] = edge_s[mine, :]
    wait_rows(wall, 8, r3.at[0])
    for l in range(2):
        columns = wall[pl.ds(l, 16, stride=8), :]
        for e in range(DEV):
            wide[pl.ds(16 * (16 * l + e), 16), :] = jnp.broadcast_to(columns[:, e : e + 1], (16, LANES))

    for u in range(1, len(UNITS) - 1):
        combine(u, *UNITS[u])
    wait_rows(stack, 8 * UNITS[-1][1], r2.at[len(UNITS) - 1])
    wait_rows(edge_r, 8, r3.at[3])
    products(*UNITS[-1])

    edge = [edge_r[pl.ds(8 * j, 8), :] for j in range(DEV)]
    turned_edge = [jnp.where(lane % 8 < 4, pltpu.roll(v, 124, 1), pltpu.roll(v, 4, 1)) for v in edge]
    for p, (l, j) in enumerate(PAIRS):
        cross[pl.ds(8 * p, 8), pl.ds(0, 128)] = edge[j - l] * edge[j]
        cross[pl.ds(8 * p, 8), pl.ds(128, 128)] = edge[j - l] * turned_edge[j]
    border[...] = dot(jnp.concatenate(halves(cross[...]), axis=1), pool[pl.ds(512 * CHUNKS, 512), :])

    above = s < DEV - 1

    @pl.when(above)
    def _():
        low_copy.wait_recv()

    low_r[...] = jnp.where(above, pltpu.roll(low_r[...], 112, 1), 0.0)
    last_look = lane % 16 == 15
    corner = (row8 == 7) & (lane % 64 >= 48)
    for p in range(len(PAIRS)):
        v = look[pl.ds(8 * p, 8), :]
        after = pltpu.roll(v, 63, 1)
        after = jnp.where(last_look, border[pl.ds(8 * p, 8), :], after)
        up = jnp.where(row8 == 0, pltpu.roll(v, 48, 1), pltpu.roll(v, 64, 1))
        up = pltpu.roll(up, 7, 0)
        up = jnp.where(corner, jnp.broadcast_to(low_r[pl.ds(p, 1), :], (8, LANES)), up)
        w = v * -half
        azim, rang = w * after, w * up
        slope[pl.ds(8 * p, 8), :] = jnp.where(lane < 64, azim, rang) + pltpu.roll(
            jnp.where(lane < 64, rang, azim), 64, 1
        )

    total = [None] * DEV
    for p, (l, j) in enumerate(PAIRS):
        v = slope[pl.ds(8 * p, 8), :]
        for e in range(DEV):
            term = wide[pl.ds(16 * (16 * (l - 1) + e) + j, 1), :] * v
            total[e] = term if total[e] is None else total[e] + term
    for e in range(DEV):
        part_s[pl.ds(8 * e, 8), :] = total[e]
    others(lambda i: part_copy(i).start())
    part_r[mine, :] = part_s[mine, :]
    wait_rows(part_r, 8, r3.at[1])

    for d in range(2):
        for h in range(CHUNKS):
            for u in range(2):
                tile = None
                for t in range(8):
                    v = part_r[pl.ds(8 * (8 * u + t), 8), :]
                    shift = 16 * (t - 4 * d - h) % 128
                    v = pltpu.roll(v, shift, 1) if shift else v
                    tile = v if tile is None else jnp.where(lane // 16 == t, v, tile)
                out[0, d, pl.ds(8 * h, 8), pl.ds(128 * u, 128)] = tile

    wait_rows(got, 128, s1.at[0], 2 * ZS - 2)
    wait_rows(flip_s, 128, s4.at[0], ZS)
    wait_rows(scene, 128, s2.at[0])
    wait_rows(wall, 8, s3.at[0])
    wait_rows(part_s, 8, s3.at[1])
    wait_rows(edge_s, 8, s3.at[3])

    @pl.when(s > 0)
    def _():
        low_copy.wait_send()


def per_device(raw_echoes, range_filter, azimuth_filter, pair_mask, inversion):
    consts = tables()
    hbm = pl.BlockSpec(memory_space=pl.ANY)
    vmem = lambda *shape: pltpu.VMEM(shape, F32)
    dma = pltpu.SemaphoreType.DMA
    return pl.pallas_call(
        kernel,
        out_shape=pltpu.VMEM((1, 2, WIDE, 256), F32),
        in_specs=[hbm] * 5 + [hbm] * len(consts),
        out_specs=pl.BlockSpec(memory_space=pltpu.VMEM),
        scratch_shapes=[vmem(2, 64, 2048), vmem(2, 2048), vmem(2, 1024, 128), vmem(2, DEV), pltpu.SMEM((1, 2), jnp.int32)]
        + [pltpu.VMEM(c.shape, c.dtype) for c in consts]
        + [
            vmem(1024, 256), vmem(32, 256), vmem(2048, 128), vmem(1024, 128), vmem(1024, 128), vmem(1024, 128), vmem(2048, 128),
            vmem(2048, 128), vmem(2048, 128), vmem(2048, 128), vmem(2048, 128),
            vmem(ROWS, 256), vmem(ROWS, 256), vmem(ROWS, 128),
            vmem(8, 128), vmem(128, 128), vmem(512, 128), vmem(128, 128), vmem(128, 128), vmem(ROWS, 128), vmem(32, 128), vmem(32, 128),
            vmem(ROWS, 128), vmem(128, 128), vmem(128, 128),
            dma((12,)), dma((8,)), dma((1,)), dma((len(UNITS),)), dma((1,)), dma((len(UNITS),)), dma((4,)), dma((4,)), dma((1,)), dma((len(UNITS),)),
        ],
        compiler_params=pltpu.CompilerParams(collective_id=0, has_side_effects=True, vmem_limit_bytes=60 * 1024 * 1024),
    )(raw_echoes, range_filter, azimuth_filter, inversion[:, 0, :].T, pair_mask, *[jnp.asarray(c) for c in consts])


def solution(mesh):
    return jax.shard_map(
        per_device,
        mesh=mesh,
        in_specs=(
            P("acq", None, "strip", None),
            P(),
            P(None, None, "strip"),
            P("acq", None),
            P(None, "acq", None),
        ),
        out_specs=P("acq", None, "strip", None),
        check_vma=False,
    )
```
